256 devices in a mesh: lon: 16 (over x_lo, y, core), rep: 16 (over z, x_hi).
Axes of the slice: x: 4 (x_hi: 2, x_lo: 2; x = x_hi * 2 + x_lo), y: 4, z: 8, core: 2. Of those that a mesh axis runs over, the one named last changes fastest.
Arguments:
- fields: bfloat16 [256, 24, 128, 256], P('rep', None, 'lon'), may hold values from -6 to 6
- stem_weight: bfloat16 [32, 24, 4, 4], replicated, may hold values from -0.3125 to 0.3125
- mid_weight: bfloat16 [64, 32, 3, 3], replicated, may hold values from -0.375 to 0.375
- head_weight: bfloat16 [64, 64, 3, 3], replicated, may hold values from -0.25 to 0.25
- out_weight: float32 [64], replicated, may hold values from -0.75 to 0.75
- pred_cotangent: float32 [256, 32, 64], P(('rep', 'lon')), may hold values from -6 to 6
Outputs:
- prediction: float32 [256, 32, 64], P(('rep', 'lon'))
- stem_cotangent: bfloat16 [256, 32, 64, 128], P('rep', None, 'lon')
- grad_stem: float32 [32, 24, 4, 4], replicated
- grad_mid: float32 [64, 32, 3, 3], replicated
- grad_head: float32 [64, 64, 3, 3], replicated
- grad_out: float32 [64], replicated
The draws below stay inside these ranges and needn't reach their ends.
All inputs are finite; a program needn't handle non-finite values.
Results may differ from the reference program's by a relative error of at most 0.0085.
Values may be sent and summed in bfloat16 or wider, within the bound.
No kernel may reach another device: no remote copies, remote signals or barrier semaphores. Data moves between devices by JAX's collectives and lax.ppermute only.
A program may use at most 128 MiB of HBM per device.

```python
import jax
import jax.numpy as jnp
from jax import lax

C_IN = 24
C1 = 32
C2 = 64
LAT = 256
SCEN = 256
LON = 128
LONH = 64
LATH = 128
LONC = 32
LATC = 64


def steps_of(stream_key, dims, shards, smallest, top_value):
    def one(axis_at, parts):
        draws = jax.random.uniform(jax.random.fold_in(jax.random.fold_in(stream_key, 6), axis_at), (parts,), jnp.float32, smallest / len(shards), top_value / len(shards))
        return jnp.repeat(jnp.exp(draws), dims[axis_at] // parts).reshape((-1,) + (1,) * (len(dims) - axis_at - 1))

    factor_of = one(*shards[0])
    for cut in shards[1:]:
        factor_of = factor_of * one(*cut)
    return factor_of


def gaussian(key, dims, scale, reach, cuts=(), held_as=jnp.bfloat16):
    loudness = steps_of(key, dims, cuts, -0.22, 0.18) if cuts else 1.0
    drawn = jax.random.normal(key, dims, jnp.float32) * scale * loudness
    return jnp.minimum(jnp.maximum(drawn, -reach), reach).astype(held_as)


def setup_inputs(seed: int = 0) -> dict:
    streams_of = jax.random.split(jax.random.key(seed), 7)
    return {
        "fields": gaussian(streams_of[0], (SCEN, C_IN, LON, LAT), 1.0, 6.0, ((0, 16), (2, 16))),
        "stem_weight": gaussian(streams_of[1], (C1, C_IN, 4, 4), (C_IN * 16) ** -0.5, 0.3125),
        "mid_weight": gaussian(streams_of[2], (C2, C1, 3, 3), (C1 * 9) ** -0.5, 0.375),
        "head_weight": gaussian(streams_of[3], (C2, C2, 3, 3), (C2 * 9) ** -0.5, 0.25),
        "out_weight": gaussian(streams_of[4], (C2,), C2 ** -0.5, 0.75, (), jnp.float32),
        "pred_cotangent": gaussian(streams_of[5], (SCEN, LONC, LATC), 1.0, 6.0, ((0, 256),), jnp.float32),
    }


exact_mode = lax.Precision.HIGHEST

def window(padded, tap_row, tap_col, out_rows, out_cols, stride):
    upper_corner = (padded.shape[0], padded.shape[1], tap_row + stride * (out_rows - 1) + 1, tap_col + stride * (out_cols - 1) + 1)
    return lax.slice(padded, (0, 0, tap_row, tap_col), upper_corner, (1, 1, stride, stride))

def conv_forward(padded, weight, stride, out_rows, out_cols):
    summed = None
    for tap_row in range(weight.shape[2]):
        for tap_col in range(weight.shape[3]):
            inputs = window(padded, tap_row, tap_col, out_rows, out_cols, stride)
            partial_term = jnp.einsum('sihw,oi->sohw', inputs, weight[:, :, tap_row, tap_col], precision=exact_mode)
            summed = partial_term if summed is None else summed + partial_term
    return summed

def conv_weight_grad(padded, cotangent, kernel, stride):
    out_rows, out_cols = (cotangent.shape[2], cotangent.shape[3])
    stacked_rows = []
    for tap_row in range(kernel):
        across = []
        for tap_col in range(kernel):
            inputs = window(padded, tap_row, tap_col, out_rows, out_cols, stride)
            across.append(jnp.einsum('sohw,sihw->oi', cotangent, inputs, precision=exact_mode))
        stacked_rows.append(jnp.stack(across, 2))
    return jnp.stack(stacked_rows, 2)

def conv_input_grad(cotangent, weight, stride, padded_shape):
    out_rows, out_cols = (cotangent.shape[2], cotangent.shape[3])
    gradient = jnp.zeros(padded_shape, jnp.float32)
    for tap_row in range(weight.shape[2]):
        for tap_col in range(weight.shape[3]):
            spread = jnp.einsum('sohw,oi->sihw', cotangent, weight[:, :, tap_row, tap_col], precision=exact_mode)
            gradient = gradient.at[:, :, tap_row:tap_row + stride * (out_rows - 1) + 1:stride, tap_col:tap_col + stride * (out_cols - 1) + 1:stride].add(spread)
    return gradient

def slope(values):
    sigma = jax.nn.sigmoid(values)
    return sigma * (1.0 + values * (1.0 - sigma))

def lat_pad(field, before, after):
    return jnp.pad(field, ((0, 0), (0, 0), (0, 0), (before, after)))

def to_half(values):
    return lax.optimization_barrier(values.astype(jnp.bfloat16))

def reference(fields, stem_weight, mid_weight, head_weight, out_weight, pred_cotangent):
    stem_full = stem_weight.astype(jnp.float32)
    mid_full = mid_weight.astype(jnp.float32)
    head_full = head_weight.astype(jnp.float32)

    def one_scenario(totals, inputs):
        field_one, cot_one = inputs
        field_one = field_one[None].astype(jnp.float32)
        cot_one = cot_one[None]
        padded_fields = lat_pad(jnp.concatenate([field_one[:, :, -1:], field_one, field_one[:, :, :1]], 2), 1, 1)
        stem_pre = conv_forward(padded_fields, stem_full, 2, LONH, LATH)
        stem_act = to_half(jax.nn.silu(stem_pre)).astype(jnp.float32)
        mid_padded = lat_pad(jnp.concatenate([stem_act[:, :, -1:], stem_act], 2), 1, 0)
        mid_pre = conv_forward(mid_padded, mid_full, 2, LONC, LATC)
        mid_act = to_half(jax.nn.silu(mid_pre)).astype(jnp.float32)
        head_padded = lat_pad(jnp.concatenate([mid_act[:, :, -1:], mid_act, mid_act[:, :, :1]], 2), 1, 1)
        head_pre = conv_forward(head_padded, head_full, 1, LONC, LATC)
        head_act = to_half(jax.nn.silu(head_pre)).astype(jnp.float32)
        prediction = jnp.einsum('c,schw->shw', out_weight, head_act, precision=exact_mode)
        head_cot = to_half(cot_one[:, None] * out_weight[None, :, None, None] * slope(head_pre)).astype(jnp.float32)
        out_sum = jnp.einsum('shw,schw->c', cot_one, head_act, precision=exact_mode)
        head_sum = conv_weight_grad(head_padded, head_cot, 3, 1)
        head_spread = conv_input_grad(head_cot, head_full, 1, head_padded.shape)
        mid_grad = head_spread[:, :, 1:-1, 1:-1]
        mid_grad = mid_grad.at[:, :, -1].add(head_spread[:, :, 0, 1:-1]).at[:, :, 0].add(head_spread[:, :, -1, 1:-1])
        mid_grad = to_half(mid_grad).astype(jnp.float32)
        mid_cot = to_half(mid_grad * slope(mid_pre)).astype(jnp.float32)
        mid_sum = conv_weight_grad(mid_padded, mid_cot, 3, 2)
        mid_spread = conv_input_grad(mid_cot, mid_full, 2, mid_padded.shape)
        stem_grad = mid_spread[:, :, 1:, 1:].at[:, :, -1].add(mid_spread[:, :, 0, 1:])
        stem_grad = to_half(stem_grad).astype(jnp.float32)
        stem_cot = (stem_grad * slope(stem_pre)).astype(jnp.bfloat16)
        stem_sum = conv_weight_grad(padded_fields, stem_cot.astype(jnp.float32), 4, 2)
        new_totals = (totals[0] + stem_sum, totals[1] + mid_sum, totals[2] + head_sum, totals[3] + out_sum)
        return (new_totals, (prediction[0], stem_cot[0]))
    initial = (jnp.zeros((C1, C_IN, 4, 4), jnp.float32), jnp.zeros((C2, C1, 3, 3), jnp.float32), jnp.zeros((C2, C2, 3, 3), jnp.float32), jnp.zeros((C2,), jnp.float32))
    totals, (prediction, stem_cotangent) = lax.scan(one_scenario, initial, (fields, pred_cotangent))
    factor = 1.0 / SCEN
    return (prediction, stem_cotangent, totals[0] * factor, totals[1] * factor, totals[2] * factor, totals[3] * factor)
```

```python
import jax
import jax.numpy as jnp
from jax import lax
from jax.sharding import PartitionSpec as P


def conv_forward(padded, weight, stride):
    return lax.conv_general_dilated(
        padded,
        weight,
        (stride, stride),
        "VALID",
        dimension_numbers=("NCHW", "OIHW", "NCHW"),
        preferred_element_type=jnp.float32,
    )


def conv_weight_grad(padded, cotangent, kernel, stride):
    out_rows, out_cols = (cotangent.shape[2], cotangent.shape[3])
    reach_rows = stride * (out_rows - 1) + kernel
    reach_cols = stride * (out_cols - 1) + kernel
    used = padded[:, :, :reach_rows, :reach_cols]
    return lax.conv_general_dilated(
        used,
        cotangent,
        (1, 1),
        "VALID",
        rhs_dilation=(stride, stride),
        dimension_numbers=("CNHW", "IOHW", "CNHW"),
        preferred_element_type=jnp.float32,
    )


def conv_input_grad(cotangent, weight, stride, padded_shape):
    kernel = weight.shape[2]
    out_rows, out_cols = (cotangent.shape[2], cotangent.shape[3])
    high_rows = padded_shape[2] - (stride * (out_rows - 1) + 1)
    high_cols = padded_shape[3] - (stride * (out_cols - 1) + 1)
    flipped = weight[:, :, ::-1, ::-1]
    return lax.conv_general_dilated(
        cotangent,
        flipped,
        (1, 1),
        ((kernel - 1, high_rows), (kernel - 1, high_cols)),
        lhs_dilation=(stride, stride),
        dimension_numbers=("NCHW", "IOHW", "NCHW"),
        preferred_element_type=jnp.float32,
    )


def slope(values):
    sigma = jax.nn.sigmoid(values)
    return sigma * (1.0 + values * (1.0 - sigma))


def lat_pad(field, before, after):
    return jnp.pad(field, ((0, 0), (0, 0), (0, 0), (before, after)))


def head_pass(mid_act, head_weight, out_weight, pred_cotangent):
    head_padded = lat_pad(
        jnp.concatenate([mid_act[:, :, -1:], mid_act, mid_act[:, :, :1]], 2), 1, 1
    )
    head_pre = conv_forward(head_padded, head_weight, 1)
    head_act = jax.nn.silu(head_pre).astype(jnp.bfloat16)
    head_wide = head_act.astype(jnp.float32)
    prediction = jnp.einsum("c,schw->shw", out_weight, head_wide)
    head_cot = (pred_cotangent[:, None] * out_weight[None, :, None, None] * slope(head_pre)).astype(
        jnp.bfloat16
    )
    out_sum = jnp.einsum("shw,schw->c", pred_cotangent, head_wide)
    head_sum = conv_weight_grad(head_padded, head_cot, 3, 1)
    head_spread = conv_input_grad(head_cot, head_weight, 1, head_padded.shape)
    mid_grad = head_spread[:, :, 1:-1, 1:-1]
    mid_grad = (
        mid_grad.at[:, :, -1]
        .add(head_spread[:, :, 0, 1:-1])
        .at[:, :, 0]
        .add(head_spread[:, :, -1, 1:-1])
    )
    return (prediction, mid_grad.astype(jnp.bfloat16), head_sum, out_sum)


def circular(field, before, after):
    parts = [field[:, :, field.shape[2] - before :]] if before else []
    parts.append(field)
    if after:
        parts.append(field[:, :, :after])
    return jnp.concatenate(parts, 2)


def exchanged(value, axis):
    return lax.all_to_all(value, axis, split_axis=0, concat_axis=0, tiled=True)


def summed_everywhere(terms):
    sizes = [term.size for term in terms]
    total = sum(sizes)
    lon, rep = lax.axis_size("lon"), lax.axis_size("rep")
    rows = -(-total // (lon * 128))
    flat = jnp.concatenate([term.reshape(-1) for term in terms])
    flat = jnp.pad(flat, (0, lon * rows * 128 - total)).reshape(lon, rows, 128)
    share = exchanged(flat, "lon").sum(0)
    share = exchanged(jnp.broadcast_to(share[None], (rep, rows, 128)), "rep").sum(0)
    whole = exchanged(jnp.broadcast_to(share[None], (lon, rows, 128)), "lon").reshape(-1)
    out, at = [], 0
    for term, size in zip(terms, sizes):
        out.append(whole[at : at + size].reshape(term.shape))
        at += size
    return out


def local(fields, stem_weight, mid_weight, head_weight, out_weight, pred_cotangent):
    whole = lax.all_to_all(fields, "lon", split_axis=0, concat_axis=2, tiled=True)
    padded_fields = lat_pad(circular(whole, 1, 1), 1, 1)
    stem_pre = conv_forward(padded_fields, stem_weight, 2)
    stem_act = jax.nn.silu(stem_pre).astype(jnp.bfloat16)
    mid_padded = lat_pad(circular(stem_act, 1, 0), 1, 0)
    mid_pre = conv_forward(mid_padded, mid_weight, 2)
    mid_act = jax.nn.silu(mid_pre).astype(jnp.bfloat16)
    prediction, mid_grad, head_sum, out_sum = head_pass(
        mid_act, head_weight, out_weight, pred_cotangent
    )
    mid_cot = (mid_grad.astype(jnp.float32) * slope(mid_pre)).astype(jnp.bfloat16)
    mid_sum = conv_weight_grad(mid_padded, mid_cot, 3, 2)
    mid_spread = conv_input_grad(mid_cot, mid_weight, 2, mid_padded.shape)
    stem_grad = mid_spread[:, :, 1:, 1:].at[:, :, -1].add(mid_spread[:, :, 0, 1:])
    stem_grad = stem_grad.astype(jnp.bfloat16)
    stem_cotangent = (stem_grad.astype(jnp.float32) * slope(stem_pre)).astype(jnp.bfloat16)
    stem_sum = conv_weight_grad(padded_fields, stem_cotangent, 4, 2)
    stem_cotangent = lax.all_to_all(stem_cotangent, "lon", split_axis=2, concat_axis=0, tiled=True)
    stem_sum, mid_sum, head_sum, out_sum = summed_everywhere(
        [stem_sum, mid_sum, head_sum, out_sum]
    )
    factor = 1.0 / (fields.shape[0] * lax.axis_size("rep"))
    return (
        prediction,
        stem_cotangent,
        stem_sum * factor,
        mid_sum * factor,
        head_sum * factor,
        out_sum * factor,
    )


def solution(mesh):
    placed = (P("rep", None, "lon", None), P(), P(), P(), P(), P(("rep", "lon"), None, None))
    return jax.shard_map(
        local,
        mesh=mesh,
        in_specs=placed,
        out_specs=(P(("rep", "lon"), None, None), P("rep", None, "lon", None), P(), P(), P(), P()),
        check_vma=False,
    )
```

```python
import jax
import jax.numpy as jnp
from jax import lax
from jax.experimental import pallas as pl
from jax.experimental.pallas import tpu as pltpu
from jax.sharding import PartitionSpec as P

BF16, F32 = jnp.bfloat16, jnp.float32
SLABS, CIN, SLAB_LON, LAT = 16, 24, 8, 256
C1, C2 = 32, 64
STEM_GROUP, MID_GROUP, HEAD_GROUP = 4, 2, 2


def one_hot(shape, test):
    rows = lax.broadcasted_iota(jnp.int32, shape, 0)
    cols = lax.broadcasted_iota(jnp.int32, shape, 1)
    return jnp.where(test(rows, cols), 1.0, 0.0).astype(BF16)


def selections():
    regroup = one_hot(
        (CIN * SLAB_LON, CIN * SLAB_LON),
        lambda r, c: (r % CIN == c // SLAB_LON) & (r // CIN == c % SLAB_LON),
    )
    field_taps = one_hot((LAT, 512), lambda r, c: r == 2 * (c % 128) + c // 128 - 1)
    stem_taps = one_hot(
        (256, 384),
        lambda r, c: (r // 128 == c % 128 // 64) & (r % 128 == 2 * (c % 64) + c // 128 - 1),
    )
    interleave = one_hot(
        (256, 256),
        lambda r, c: (r % 128 // 64 == c // 128) & (c % 128 == 2 * (r % 64) + r // 128),
    )
    slab_rows = one_hot((128, 128), lambda r, c: (r % 4 == c // C1) & (r // 4 == c % C1))
    return regroup, field_taps, stem_taps, interleave, slab_rows


def toeplitz(rows, group, step):
    out, window, depth = rows.shape
    width = step * (group - 1) + window
    copies = [
        jnp.pad(rows, ((0, 0), (step * at, width - window - step * at), (0, 0))) for at in range(group)
    ]
    return jnp.stack(copies).reshape(group * out, width * depth)


def kernel_weights(stem_weight, mid_weight, head_weight):
    stem = stem_weight.transpose(0, 2, 3, 1).reshape(C1, 4, 4 * CIN)
    mid = mid_weight.transpose(0, 2, 3, 1).reshape(C2, 3, 3 * C1)
    head = head_weight.transpose(0, 2, 3, 1).reshape(C2, 3, 3 * C2)
    head_back = head_weight[:, :, ::-1, ::-1].transpose(1, 2, 3, 0).reshape(C2, 3, 3 * C2)
    none = jnp.zeros((C1, C2), mid_weight.dtype)
    blocks = []
    for lat_odd in (0, 1):
        for lon_odd in (0, 1):
            row = []
            for next_lon in (0, 1):
                for next_lat in (0, 1):
                    if next_lon > lon_odd or next_lat > lat_odd:
                        row.append(none)
                    else:
                        a = 1 if not lon_odd else 2 - 2 * next_lon
                        b = 1 if not lat_odd else 2 - 2 * next_lat
                        row.append(mid_weight[:, :, a, b].T)
            blocks.append(jnp.concatenate(row, 1))
    mid_back = jnp.concatenate(blocks, 0)
    return (
        toeplitz(stem, STEM_GROUP, 2),
        toeplitz(mid, MID_GROUP, 2),
        toeplitz(head, HEAD_GROUP, 1),
        toeplitz(head_back, HEAD_GROUP, 1),
        mid_back,
    )


def dot(left, right):
    return jnp.dot(left, right, preferred_element_type=F32)


def dot_t(left, right):
    return lax.dot_general(left, right, (((1,), (1,)), ((), ())), preferred_element_type=F32)


def swapped(block):
    return pltpu.roll(block.astype(F32), 64, 1).astype(BF16)


def sigmoid(values):
    return 1.0 / (1.0 + jnp.exp(-values))


def slope_of(values):
    sigma = sigmoid(values)
    return sigma * (1.0 + values * (1.0 - sigma))


def scenario_kernel(
    x_ref, w1_ref, w2_ref, w3_ref, w3b_ref, w2b_ref, regroup_ref, ftaps_ref, staps_ref, inter_ref, rows_ref,
    ow_ref, pc_ref,
    pred_ref, cot_ref, sums_ref,
    fx, stem_pre, mx, mid_pre, hx, hc_wide, hc_pad, mc_pair, mc_pad, sc_pad,
):
    lane = lax.broadcasted_iota(jnp.int32, (C2, 128), 1) % 64
    first, last = lane == 0, lane == 63

    def earlier(block):
        return jnp.where(first, 0.0, pltpu.roll(block, 1, 1))

    def later(block):
        return jnp.where(last, 0.0, pltpu.roll(block, 127, 1))

    def load_slab(s, _):
        for half in (0, 1):
            part = dot(regroup_ref[...], x_ref[s + 8 * half]).astype(BF16)
            taps = dot(part, ftaps_ref[...])
            wide = jnp.concatenate(
                [taps[:, 128 * b : 128 * b + 128].reshape(SLAB_LON, CIN, 128) for b in range(4)], 1
            )
            fx[pl.ds(1 + s * SLAB_LON, SLAB_LON), :, half * 128 : half * 128 + 128] = wide.astype(BF16)
        return 0

    lax.fori_loop(0, 8, load_slab, 0)
    fx[0, :, 0:128] = fx[64, :, 128:256]
    fx[0, :, 128:256] = fx[64, :, 0:128]
    fx[65, :, 0:128] = fx[1, :, 128:256]
    fx[65, :, 128:256] = fx[1, :, 0:128]

    def stem(g, _):
        n = STEM_GROUP
        window = fx[pl.ds(2 * n * g, 2 * n + 2)].reshape((2 * n + 2) * 96, 256)
        pre = dot(w1_ref[...], window)
        stem_pre[pl.ds(n * g, n)] = pre.reshape(n, C1, 256)
        act = (pre * sigmoid(pre)).astype(BF16)
        taps = dot(act, staps_ref[...])
        wide = jnp.concatenate([taps[:, 128 * b : 128 * b + 128].reshape(n, C1, 128) for b in range(3)], 1)
        mx[pl.ds(1 + n * g, n)] = wide.astype(BF16)
        return 0

    lax.fori_loop(0, 32 // STEM_GROUP, stem, 0)
    mx[0] = swapped(mx[32])
    mx[33] = jnp.zeros((96, 128), BF16)

    def mid(g, _):
        n = MID_GROUP
        window = mx[pl.ds(2 * n * g, 2 * n + 1)].reshape((2 * n + 1) * 96, 128)
        pre = dot(w2_ref[...], window)
        mid_pre[pl.ds(n * g, n)] = pre.reshape(n, C2, 128)
        act = pre * sigmoid(pre)
        for k in range(n):
            one = act[k * C2 : k * C2 + C2]
            hx[n * g + k + 1] = jnp.concatenate([earlier(one), one, later(one)], 0).astype(BF16)
        return 0

    lax.fori_loop(0, 16 // MID_GROUP, mid, 0)
    hx[0] = swapped(hx[16])
    hx[17] = swapped(hx[1])

    for edge in (0, 1, 18, 19):
        hc_pad[edge] = jnp.zeros((C2, 128), BF16)
    out_w = jnp.broadcast_to(ow_ref[...], (C2, 128))

    def head(g, out_sum):
        n = HEAD_GROUP
        window = hx[pl.ds(n * g, n + 2)].reshape((n + 2) * 192, 128)
        pre = dot(w3_ref[...], window)
        sigma = sigmoid(pre)
        act = (pre * sigma).astype(BF16).astype(F32)
        bend = sigma * (1.0 + pre * (1.0 - sigma))
        for k in range(n):
            r = n * g + k
            here = slice(k * C2, k * C2 + C2)
            cot = jnp.broadcast_to(pc_ref[pl.ds(r, 1), :], (C2, 128))
            pred_ref[pl.ds(r, 1), :] = jnp.sum(out_w * act[here], 0, keepdims=True)
            out_sum = out_sum + cot * act[here]
            hc = (cot * out_w) * bend[here]
            hc_pad[r + 2] = hc.astype(BF16)
            hc_wide[r + 1] = jnp.concatenate([earlier(hc), hc, later(hc)], 0).astype(BF16)
        return out_sum

    out_sum = lax.fori_loop(0, 16 // HEAD_GROUP, head, jnp.zeros((C2, 128), F32))
    sums_ref[576:640, :] = out_sum
    hc_wide[0] = swapped(hc_wide[16])
    hc_wide[17] = swapped(hc_wide[1])

    for edge in (0, 17):
        mc_pad[edge] = jnp.zeros((C2, 128), BF16)

    def head_back(g, _):
        n = HEAD_GROUP
        window = hc_wide[pl.ds(n * g, n + 2)].reshape((n + 2) * 192, 128)
        grad = dot(w3b_ref[...], window).astype(BF16).astype(F32)
        mc = grad * slope_of(mid_pre[pl.ds(n * g, n)].reshape(n * C2, 128))
        for k in range(n):
            one = mc[k * C2 : k * C2 + C2]
            mc_pad[n * g + k + 1] = one.astype(BF16)
            mc_pair[n * g + k] = jnp.concatenate([one, later(one)], 0).astype(BF16)
        return 0

    lax.fori_loop(0, 16 // HEAD_GROUP, head_back, 0)
    mc_pair[16] = swapped(mc_pair[0])

    for edge in (0, 33):
        sc_pad[edge] = jnp.zeros((C1, 256), BF16)

    def mid_back(m, _):
        parts = []
        for k in range(2):
            window = mc_pair[pl.ds(2 * m + k, 2)].reshape(256, 128)
            grad = dot(w2b_ref[...], window).astype(BF16)
            parts.append(jnp.concatenate([grad[0:64], grad[64:128]], 1))
        grad = dot(jnp.concatenate(parts, 0), inter_ref[...])
        cot = (grad * slope_of(stem_pre[pl.ds(4 * m, 4)].reshape(128, 256))).astype(BF16)
        sc_pad[pl.ds(4 * m + 1, 4)] = cot.reshape(4, C1, 256)
        out = dot(rows_ref[...], cot).astype(BF16)
        cot_ref[m] = out[:, 0:128]
        cot_ref[m + 8] = out[:, 128:256]
        return 0

    lax.fori_loop(0, 8, mid_back, 0)

    def head_sum(p, total):
        left = jnp.concatenate([hc_pad[pl.ds(2 * p + k, 3)].reshape(192, 128) for k in range(2)], 1)
        right = jnp.concatenate([hx[2 * p], hx[2 * p + 1]], 1)
        return total + dot_t(left, right)

    total = lax.fori_loop(0, 9, head_sum, jnp.zeros((192, 192), F32))
    sums_ref[0:192, :] = total[:, 0:128]
    sums_ref[192:384, 0:64] = total[:, 128:192]

    def mid_sum(m, total):
        return total + dot_t(mx[pl.ds(2 * m, 2)].reshape(192, 128), mc_pad[pl.ds(m, 2)].reshape(128, 128))

    sums_ref[384:576, :] = lax.fori_loop(0, 17, mid_sum, jnp.zeros((192, 128), F32))

    def stem_sum(m, total):
        return total + dot_t(fx[pl.ds(2 * m, 2)].reshape(192, 256), sc_pad[pl.ds(m, 2)].reshape(64, 256))

    sums_ref[192:384, 64:128] = lax.fori_loop(0, 33, stem_sum, jnp.zeros((192, 64), F32))


def scenario_pass(x, weights, out_weight, cotangent):
    out_shape = (
        jax.ShapeDtypeStruct((16, 128), F32),
        jax.ShapeDtypeStruct((SLABS, 128, 128), BF16),
        jax.ShapeDtypeStruct((640, 128), F32),
    )
    scratch = [
        pltpu.VMEM((66, 96, 256), BF16),
        pltpu.VMEM((32, C1, 256), F32),
        pltpu.VMEM((34, 96, 128), BF16),
        pltpu.VMEM((16, C2, 128), F32),
        pltpu.VMEM((18, 192, 128), BF16),
        pltpu.VMEM((18, 192, 128), BF16),
        pltpu.VMEM((20, C2, 128), BF16),
        pltpu.VMEM((17, 128, 128), BF16),
        pltpu.VMEM((18, C2, 128), BF16),
        pltpu.VMEM((34, C1, 256), BF16),
    ]
    whole = pl.BlockSpec(memory_space=pltpu.VMEM)
    return pl.pallas_call(
        scenario_kernel,
        out_shape=out_shape,
        in_specs=[whole] * 13,
        out_specs=(whole,) * 3,
        scratch_shapes=scratch,
        compiler_params=pltpu.CompilerParams(vmem_limit_bytes=48 << 20),
        cost_estimate=pl.CostEstimate(flops=4 * 10**9, bytes_accessed=4 << 20, transcendentals=10**6),
        name="scenario",
    )(x, *weights, *selections(), out_weight.reshape(C2, 1), cotangent)


def exchanged(value, axis):
    return lax.all_to_all(value, axis, split_axis=0, concat_axis=0, tiled=True)


def summed_everywhere(terms):
    lon, rep = lax.axis_size("lon"), lax.axis_size("rep")
    shape = (terms.shape[0] // lon, 128)
    share = exchanged(terms.reshape(lon, *shape), "lon").sum(0)
    share = exchanged(jnp.broadcast_to(share[None], (rep, *shape)), "rep").sum(0)
    return exchanged(jnp.broadcast_to(share[None], (lon, *shape)), "lon").reshape(terms.shape)


def unpacked(sums):
    head = jnp.concatenate([sums[0:192], sums[192:384, 0:64]], 1)
    head = head.reshape(3, C2, 3, C2)[::-1].transpose(1, 3, 0, 2)
    mid = sums[384:576].reshape(2, 3, C1, 2, C2)
    mid = jnp.stack([mid[0, :, :, 1], mid[1, :, :, 1], mid[0, :, :, 0]])
    stem = sums[192:384, 64:128].reshape(2, 4, CIN, 2, C1)
    stem = jnp.stack([stem[0, :, :, 1], stem[1, :, :, 1], stem[0, :, :, 0], stem[1, :, :, 0]])
    return stem.transpose(3, 2, 0, 1), mid.transpose(3, 2, 0, 1), head, sums[576:640].sum(1)


def local(fields, stem_weight, mid_weight, head_weight, out_weight, pred_cotangent):
    x = exchanged(fields.reshape(SLABS, CIN * SLAB_LON, LAT), "lon")
    weights = kernel_weights(stem_weight, mid_weight, head_weight)
    cotangent = pred_cotangent.reshape(2, 16, 64).transpose(1, 0, 2).reshape(16, 128)
    prediction, stem_cotangent, sums = scenario_pass(x, weights, out_weight, cotangent)
    prediction = prediction.reshape(16, 2, 64).transpose(1, 0, 2).reshape(1, 32, 64)
    stem_cotangent = exchanged(stem_cotangent, "lon").reshape(SLABS, C1, 4, 128)
    grads = unpacked(summed_everywhere(sums))
    factor = 1.0 / (fields.shape[0] * lax.axis_size("rep"))
    return (prediction, stem_cotangent, *(grad * factor for grad in grads))


def solution(mesh):
    placed = (P("rep", None, "lon", None), P(), P(), P(), P(), P(("rep", "lon"), None, None))
    return jax.shard_map(
        local,
        mesh=mesh,
        in_specs=placed,
        out_specs=(P(("rep", "lon"), None, None), P("rep", None, "lon", None), P(), P(), P(), P()),
        check_vma=False,
    )
```

```python
import functools

import jax
import jax.numpy as jnp
from jax import lax
from jax.experimental import pallas as pl
from jax.experimental.pallas import tpu as pltpu
from jax.sharding import PartitionSpec as P

BF16, F32 = jnp.bfloat16, jnp.float32
SLABS, CIN, SLAB_LON, LAT = 16, 24, 8, 256
C1, C2 = 32, 64
COT_ROWS, SHARE = 128, 40
WIRE_ROWS = COT_ROWS + 2 * SHARE
STEM_GROUP, MID_GROUP, HEAD_GROUP = 4, 2, 2


def one_hot(shape, test):
    rows = lax.broadcasted_iota(jnp.int32, shape, 0)
    cols = lax.broadcasted_iota(jnp.int32, shape, 1)
    return jnp.where(test(rows, cols), 1.0, 0.0).astype(BF16)


def selections():
    regroup = one_hot(
        (CIN * SLAB_LON, CIN * SLAB_LON),
        lambda r, c: (r % CIN == c // SLAB_LON) & (r // CIN == c % SLAB_LON),
    )
    field_taps = one_hot((LAT, 512), lambda r, c: r == 2 * (c % 128) + c // 128 - 1)
    stem_taps = one_hot(
        (256, 384),
        lambda r, c: (r // 128 == c % 128 // 64) & (r % 128 == 2 * (c % 64) + c // 128 - 1),
    )
    interleave = one_hot(
        (256, 256),
        lambda r, c: (r % 128 // 64 == c // 128) & (c % 128 == 2 * (r % 64) + r // 128),
    )
    slab_rows = one_hot((128, 128), lambda r, c: (r % 4 == c // C1) & (r // 4 == c % C1))
    return regroup, field_taps, stem_taps, interleave, slab_rows


def toeplitz(rows, group, step):
    out, window, depth = rows.shape
    width = step * (group - 1) + window
    copies = [
        jnp.pad(rows, ((0, 0), (step * at, width - window - step * at), (0, 0))) for at in range(group)
    ]
    return jnp.stack(copies).reshape(group * out, width * depth)


def kernel_weights(stem_weight, mid_weight, head_weight):
    stem = stem_weight.transpose(0, 2, 3, 1).reshape(C1, 4, 4 * CIN)
    mid = mid_weight.transpose(0, 2, 3, 1).reshape(C2, 3, 3 * C1)
    head = head_weight.transpose(0, 2, 3, 1).reshape(C2, 3, 3 * C2)
    head_back = head_weight[:, :, ::-1, ::-1].transpose(1, 2, 3, 0).reshape(C2, 3, 3 * C2)
    none = jnp.zeros((C1, C2), mid_weight.dtype)
    blocks = []
    for lat_odd in (0, 1):
        for lon_odd in (0, 1):
            row = []
            for next_lon in (0, 1):
                for next_lat in (0, 1):
                    if next_lon > lon_odd or next_lat > lat_odd:
                        row.append(none)
                    else:
                        a = 1 if not lon_odd else 2 - 2 * next_lon
                        b = 1 if not lat_odd else 2 - 2 * next_lat
                        row.append(mid_weight[:, :, a, b].T)
            blocks.append(jnp.concatenate(row, 1))
    mid_back = jnp.concatenate(blocks, 0)
    return (
        toeplitz(stem, STEM_GROUP, 2),
        toeplitz(mid, MID_GROUP, 2),
        toeplitz(head, HEAD_GROUP, 1),
        toeplitz(head_back, HEAD_GROUP, 1),
        mid_back,
    )


def dot(left, right):
    return jnp.dot(left, right, preferred_element_type=F32)


def dot_t(left, right):
    return lax.dot_general(left, right, (((1,), (1,)), ((), ())), preferred_element_type=F32)


def swapped(block):
    return pltpu.roll(block.astype(F32), 64, 1).astype(BF16)


def sigmoid(values):
    return 1.0 / (1.0 + jnp.exp(-values))


def slope_of(values):
    sigma = sigmoid(values)
    return sigma * (1.0 + values * (1.0 - sigma))


def scenario_kernel(
    x_ref, w1_ref, w2_ref, w3_ref, w3b_ref, w2b_ref, regroup_ref, ftaps_ref, staps_ref, inter_ref, rows_ref,
    ow_ref, pc_ref,
    pred_ref, wire_ref,
    sums_ref, fx, stem_pre, mx, mid_pre, hx, hc_wide, hc_pad, mc_pair, mc_pad, sc_pad,
):
    lane = lax.broadcasted_iota(jnp.int32, (C2, 128), 1) % 64
    first, last = lane == 0, lane == 63

    def earlier(block):
        return jnp.where(first, 0.0, pltpu.roll(block, 1, 1))

    def later(block):
        return jnp.where(last, 0.0, pltpu.roll(block, 127, 1))

    def load_slab(s, _):
        for half in (0, 1):
            part = dot(regroup_ref[...], x_ref[s + 8 * half]).astype(BF16)
            taps = dot(part, ftaps_ref[...])
            wide = jnp.concatenate(
                [taps[:, 128 * b : 128 * b + 128].reshape(SLAB_LON, CIN, 128) for b in range(4)], 1
            )
            fx[pl.ds(1 + s * SLAB_LON, SLAB_LON), :, half * 128 : half * 128 + 128] = wide.astype(BF16)
        return 0

    lax.fori_loop(0, 8, load_slab, 0)
    fx[0, :, 0:128] = fx[64, :, 128:256]
    fx[0, :, 128:256] = fx[64, :, 0:128]
    fx[65, :, 0:128] = fx[1, :, 128:256]
    fx[65, :, 128:256] = fx[1, :, 0:128]

    def stem(g, _):
        n = STEM_GROUP
        window = fx[pl.ds(2 * n * g, 2 * n + 2)].reshape((2 * n + 2) * 96, 256)
        pre = dot(w1_ref[...], window)
        stem_pre[pl.ds(n * g, n)] = pre.reshape(n, C1, 256)
        act = (pre * sigmoid(pre)).astype(BF16)
        taps = dot(act, staps_ref[...])
        wide = jnp.concatenate([taps[:, 128 * b : 128 * b + 128].reshape(n, C1, 128) for b in range(3)], 1)
        mx[pl.ds(1 + n * g, n)] = wide.astype(BF16)
        return 0

    lax.fori_loop(0, 32 // STEM_GROUP, stem, 0)
    mx[0] = swapped(mx[32])
    mx[33] = jnp.zeros((96, 128), BF16)

    def mid(g, _):
        n = MID_GROUP
        window = mx[pl.ds(2 * n * g, 2 * n + 1)].reshape((2 * n + 1) * 96, 128)
        pre = dot(w2_ref[...], window)
        mid_pre[pl.ds(n * g, n)] = pre.reshape(n, C2, 128)
        act = pre * sigmoid(pre)
        for k in range(n):
            one = act[k * C2 : k * C2 + C2]
            hx[n * g + k + 1] = jnp.concatenate([earlier(one), one, later(one)], 0).astype(BF16)
        return 0

    lax.fori_loop(0, 16 // MID_GROUP, mid, 0)
    hx[0] = swapped(hx[16])
    hx[17] = swapped(hx[1])

    for edge in (0, 1, 18, 19):
        hc_pad[edge] = jnp.zeros((C2, 128), BF16)
    out_w = jnp.broadcast_to(ow_ref[...], (C2, 128))

    def head(g, out_sum):
        n = HEAD_GROUP
        window = hx[pl.ds(n * g, n + 2)].reshape((n + 2) * 192, 128)
        pre = dot(w3_ref[...], window)
        sigma = sigmoid(pre)
        act = (pre * sigma).astype(BF16).astype(F32)
        bend = sigma * (1.0 + pre * (1.0 - sigma))
        for k in range(n):
            r = n * g + k
            here = slice(k * C2, k * C2 + C2)
            cot = jnp.broadcast_to(pc_ref[pl.ds(r, 1), :], (C2, 128))
            pred_ref[pl.ds(r, 1), :] = jnp.sum(out_w * act[here], 0, keepdims=True)
            out_sum = out_sum + cot * act[here]
            hc = (cot * out_w) * bend[here]
            hc_pad[r + 2] = hc.astype(BF16)
            hc_wide[r + 1] = jnp.concatenate([earlier(hc), hc, later(hc)], 0).astype(BF16)
        return out_sum

    out_sum = lax.fori_loop(0, 16 // HEAD_GROUP, head, jnp.zeros((C2, 128), F32))
    sums_ref[576:640, :] = out_sum
    hc_wide[0] = swapped(hc_wide[16])
    hc_wide[17] = swapped(hc_wide[1])

    for edge in (0, 17):
        mc_pad[edge] = jnp.zeros((C2, 128), BF16)

    def head_back(g, _):
        n = HEAD_GROUP
        window = hc_wide[pl.ds(n * g, n + 2)].reshape((n + 2) * 192, 128)
        grad = dot(w3b_ref[...], window).astype(BF16).astype(F32)
        mc = grad * slope_of(mid_pre[pl.ds(n * g, n)].reshape(n * C2, 128))
        for k in range(n):
            one = mc[k * C2 : k * C2 + C2]
            mc_pad[n * g + k + 1] = one.astype(BF16)
            mc_pair[n * g + k] = jnp.concatenate([one, later(one)], 0).astype(BF16)
        return 0

    lax.fori_loop(0, 16 // HEAD_GROUP, head_back, 0)
    mc_pair[16] = swapped(mc_pair[0])

    for edge in (0, 33):
        sc_pad[edge] = jnp.zeros((C1, 256), BF16)

    def mid_back(m, _):
        parts = []
        for k in range(2):
            window = mc_pair[pl.ds(2 * m + k, 2)].reshape(256, 128)
            grad = dot(w2b_ref[...], window).astype(BF16)
            parts.append(jnp.concatenate([grad[0:64], grad[64:128]], 1))
        grad = dot(jnp.concatenate(parts, 0), inter_ref[...])
        cot = (grad * slope_of(stem_pre[pl.ds(4 * m, 4)].reshape(128, 256))).astype(BF16)
        sc_pad[pl.ds(4 * m + 1, 4)] = cot.reshape(4, C1, 256)
        out = dot(rows_ref[...], cot).astype(BF16)
        wire_ref[m, 0:COT_ROWS] = out[:, 0:128]
        wire_ref[m + 8, 0:COT_ROWS] = out[:, 128:256]
        return 0

    lax.fori_loop(0, 8, mid_back, 0)

    def head_sum(p, total):
        left = jnp.concatenate([hc_pad[pl.ds(2 * p + k, 3)].reshape(192, 128) for k in range(2)], 1)
        right = jnp.concatenate([hx[2 * p], hx[2 * p + 1]], 1)
        return total + dot_t(left, right)

    total = lax.fori_loop(0, 9, head_sum, jnp.zeros((192, 192), F32))
    sums_ref[0:192, :] = total[:, 0:128]
    sums_ref[192:384, 0:64] = total[:, 128:192]

    def mid_sum(m, total):
        return total + dot_t(mx[pl.ds(2 * m, 2)].reshape(192, 128), mc_pad[pl.ds(m, 2)].reshape(128, 128))

    sums_ref[384:576, :] = lax.fori_loop(0, 17, mid_sum, jnp.zeros((192, 128), F32))

    def stem_sum(m, total):
        return total + dot_t(fx[pl.ds(2 * m, 2)].reshape(192, 256), sc_pad[pl.ds(m, 2)].reshape(64, 256))

    sums_ref[192:384, 64:128] = lax.fori_loop(0, 33, stem_sum, jnp.zeros((192, 64), F32))

    for s in range(SLABS):
        term = sums_ref[s * SHARE : s * SHARE + SHARE, :]
        near = term.astype(BF16).astype(F32)
        wire_ref[s, COT_ROWS:WIRE_ROWS] = jnp.concatenate([near, term - near], 0).astype(BF16)


def scenario_pass(x, weights, out_weight, cotangent):
    out_shape = (
        jax.ShapeDtypeStruct((16, 128), F32),
        jax.ShapeDtypeStruct((SLABS, WIRE_ROWS, 128), BF16),
    )
    scratch = [
        pltpu.VMEM((SLABS * SHARE, 128), F32),
        pltpu.VMEM((66, 96, 256), BF16),
        pltpu.VMEM((32, C1, 256), F32),
        pltpu.VMEM((34, 96, 128), BF16),
        pltpu.VMEM((16, C2, 128), F32),
        pltpu.VMEM((18, 192, 128), BF16),
        pltpu.VMEM((18, 192, 128), BF16),
        pltpu.VMEM((20, C2, 128), BF16),
        pltpu.VMEM((17, 128, 128), BF16),
        pltpu.VMEM((18, C2, 128), BF16),
        pltpu.VMEM((34, C1, 256), BF16),
    ]
    whole = pl.BlockSpec(memory_space=pltpu.VMEM)
    return pl.pallas_call(
        scenario_kernel,
        out_shape=out_shape,
        in_specs=[whole] * 13,
        out_specs=(whole,) * 2,
        scratch_shapes=scratch,
        compiler_params=pltpu.CompilerParams(vmem_limit_bytes=48 << 20),
        cost_estimate=pl.CostEstimate(flops=4 * 10**9, bytes_accessed=4 << 20, transcendentals=10**6),
        name="scenario",
    )(x, *weights, *selections(), out_weight.reshape(C2, 1), cotangent)


def exchanged(value, axis):
    return lax.all_to_all(value, axis, split_axis=0, concat_axis=0, tiled=True)


def lon_share_kernel(got_ref, out_ref):
    total = jnp.zeros((2 * SHARE, 128), F32)
    for k in range(SLABS):
        total = total + got_ref[k, COT_ROWS:WIRE_ROWS].astype(F32)
    share = (total[0:SHARE] + total[SHARE : 2 * SHARE]).astype(BF16)
    for k in range(SLABS):
        out_ref[k] = share


def rep_share_kernel(got_ref, out_ref):
    total = jnp.zeros((SHARE, 128), F32)
    for k in range(SLABS):
        total = total + got_ref[k].astype(F32)
    share = total.astype(BF16)
    for k in range(SLABS):
        out_ref[k] = share


def unpack_kernel(factor, sums_ref, stem_ref, mid_ref, head_ref, out_ref, wide):
    wide[...] = sums_ref[...].astype(F32) * factor
    for a in range(3):
        at = (2 - a) * C2
        head_ref[a, 0] = wide[at : at + C2, 0:64]
        head_ref[a, 1] = wide[at : at + C2, 64:128]
        head_ref[a, 2] = wide[192 + at : 192 + at + C2, 0:64]
        lanes = slice(0, 64) if a == 2 else slice(64, 128)
        for b in range(3):
            at = 384 + a % 2 * 96 + b * C1
            mid_ref[a, b] = wide[at : at + C1, lanes]
    for a in range(4):
        lanes = slice(64, 96) if a >= 2 else slice(96, 128)
        for c in range(CIN):
            rows = wide[pl.ds(192 + a % 2 * 96 + c, 4, stride=CIN), :]
            stem_ref[c, a] = rows[:, lanes]
    ones = jnp.full((8, 128), 1.0, BF16)
    out_ref[...] = dot_t(ones, sums_ref[576:640])[0:1] * factor


def on_chip(kernel, outs, scratch=(), name=None):
    whole = pl.BlockSpec(memory_space=pltpu.VMEM)
    single = not isinstance(outs, tuple)
    return lambda *args: pl.pallas_call(
        kernel,
        out_shape=outs,
        in_specs=[whole] * len(args),
        out_specs=whole if single else (whole,) * len(outs),
        scratch_shapes=scratch,
        name=name,
    )(*args)


def summed_everywhere(got, factor):
    shares = jax.ShapeDtypeStruct((SLABS, SHARE, 128), BF16)
    share = on_chip(lon_share_kernel, shares, name="lon_share")(got)
    share = on_chip(rep_share_kernel, shares, name="rep_share")(exchanged(share, "rep"))
    sums = exchanged(share, "lon").reshape(SLABS * SHARE, 128)
    outs = (
        jax.ShapeDtypeStruct((CIN, 4, 4, C1), F32),
        jax.ShapeDtypeStruct((3, 3, C1, C2), F32),
        jax.ShapeDtypeStruct((3, 3, C2, C2), F32),
        jax.ShapeDtypeStruct((1, C2), F32),
    )
    scratch = [pltpu.VMEM((SLABS * SHARE, 128), F32)]
    stem, mid, head, out = on_chip(functools.partial(unpack_kernel, factor), outs, scratch, "unpack")(sums)
    return stem.transpose(3, 0, 1, 2), mid.transpose(3, 2, 0, 1), head.transpose(2, 3, 0, 1), out.reshape(C2)


def local(fields, stem_weight, mid_weight, head_weight, out_weight, pred_cotangent):
    x = exchanged(fields.reshape(SLABS, CIN * SLAB_LON, LAT), "lon")
    weights = kernel_weights(stem_weight, mid_weight, head_weight)
    cotangent = pred_cotangent.reshape(2, 16, 64).transpose(1, 0, 2).reshape(16, 128)
    prediction, wire = scenario_pass(x, weights, out_weight, cotangent)
    prediction = prediction.reshape(16, 2, 64).transpose(1, 0, 2).reshape(1, 32, 64)
    got = exchanged(wire, "lon")
    stem_cotangent = got[:, 0:COT_ROWS].reshape(SLABS, C1, 4, 128)
    factor = 1.0 / (fields.shape[0] * lax.axis_size("rep"))
    return (prediction, stem_cotangent, *summed_everywhere(got, factor))


def solution(mesh):
    placed = (P("rep", None, "lon", None), P(), P(), P(), P(), P(("rep", "lon"), None, None))
    return jax.shard_map(
        local,
        mesh=mesh,
        in_specs=placed,
        out_specs=(P(("rep", "lon"), None, None), P("rep", None, "lon", None), P(), P(), P(), P()),
        check_vma=False,
    )
```

```python
import functools

import jax
import jax.numpy as jnp
from jax import lax
from jax.experimental import pallas as pl
from jax.experimental.pallas import tpu as pltpu
from jax.sharding import PartitionSpec as P

BF16, F32 = jnp.bfloat16, jnp.float32
SLABS, CIN, SLAB_LON, LAT = 16, 24, 8, 256
C1, C2 = 32, 64
COT_ROWS, SHARE = 128, 40
SUM_ROWS = 2 * SHARE
WIRE_ROWS = SUM_ROWS + COT_ROWS
STEM_GROUP, MID_GROUP, HEAD_GROUP = 4, 2, 2


def one_hot(shape, test):
    rows = lax.broadcasted_iota(jnp.int32, shape, 0)
    cols = lax.broadcasted_iota(jnp.int32, shape, 1)
    return jnp.where(test(rows, cols), 1.0, 0.0).astype(BF16)


def selections():
    regroup = one_hot(
        (CIN * SLAB_LON, CIN * SLAB_LON),
        lambda r, c: (r % CIN == c // SLAB_LON) & (r // CIN == c % SLAB_LON),
    )
    field_taps = one_hot((LAT, 512), lambda r, c: r == 2 * (c % 128) + c // 128 - 1)
    stem_taps = one_hot(
        (256, 384),
        lambda r, c: (r // 128 == c % 128 // 64) & (r % 128 == 2 * (c % 64) + c // 128 - 1),
    )
    interleave = one_hot(
        (256, 256),
        lambda r, c: (r % 128 // 64 == c // 128) & (c % 128 == 2 * (r % 64) + r // 128),
    )
    slab_rows = one_hot((128, 128), lambda r, c: (r % 4 == c // C1) & (r // 4 == c % C1))
    return regroup, field_taps, stem_taps, interleave, slab_rows


def toeplitz(rows, group, step):
    out, window, depth = rows.shape
    width = step * (group - 1) + window
    copies = [
        jnp.pad(rows, ((0, 0), (step * at, width - window - step * at), (0, 0))) for at in range(group)
    ]
    return jnp.stack(copies).reshape(group * out, width * depth)


def kernel_weights(stem_weight, mid_weight, head_weight):
    stem = stem_weight.transpose(0, 2, 3, 1).reshape(C1, 4, 4 * CIN)
    mid = mid_weight.transpose(0, 2, 3, 1).reshape(C2, 3, 3 * C1)
    head = head_weight.transpose(0, 2, 3, 1).reshape(C2, 3, 3 * C2)
    head_back = head_weight[:, :, ::-1, ::-1].transpose(1, 2, 3, 0).reshape(C2, 3, 3 * C2)
    none = jnp.zeros((C1, C2), mid_weight.dtype)
    blocks = []
    for lat_odd in (0, 1):
        for lon_odd in (0, 1):
            row = []
            for next_lon in (0, 1):
                for next_lat in (0, 1):
                    if next_lon > lon_odd or next_lat > lat_odd:
                        row.append(none)
                    else:
                        a = 1 if not lon_odd else 2 - 2 * next_lon
                        b = 1 if not lat_odd else 2 - 2 * next_lat
                        row.append(mid_weight[:, :, a, b].T)
            blocks.append(jnp.concatenate(row, 1))
    mid_back = jnp.concatenate(blocks, 0)
    return (
        toeplitz(stem, STEM_GROUP, 2),
        toeplitz(mid, MID_GROUP, 2),
        toeplitz(head, HEAD_GROUP, 1),
        toeplitz(head_back, HEAD_GROUP, 1),
        mid_back,
    )


def dot(left, right):
    return jnp.dot(left, right, preferred_element_type=F32)


def dot_t(left, right):
    return lax.dot_general(left, right, (((1,), (1,)), ((), ())), preferred_element_type=F32)


def swapped(block):
    return pltpu.roll(block.astype(F32), 64, 1).astype(BF16)


def sigmoid(values):
    return 1.0 / (1.0 + jnp.exp(-values))


def slope_of(values):
    sigma = sigmoid(values)
    return sigma * (1.0 + values * (1.0 - sigma))


def scenario_kernel(
    x_ref, w1_ref, w2_ref, w3_ref, w3b_ref, w2b_ref, regroup_ref, ftaps_ref, staps_ref, inter_ref, rows_ref,
    ow_ref, pc_ref,
    pred_ref, wire_ref,
    sums_ref, fx, stem_pre, mx, mid_pre, hx, hc_wide, hc_pad, mc_pair, mc_pad, sc_pad,
):
    lane = lax.broadcasted_iota(jnp.int32, (C2, 128), 1) % 64
    first, last = lane == 0, lane == 63

    def earlier(block):
        return jnp.where(first, 0.0, pltpu.roll(block, 1, 1))

    def later(block):
        return jnp.where(last, 0.0, pltpu.roll(block, 127, 1))

    def load_slab(s):
        for half in (0, 1):
            part = dot(regroup_ref[...], x_ref[s + 8 * half]).astype(BF16)
            taps = dot(part, ftaps_ref[...])
            wide = jnp.concatenate(
                [taps[:, 128 * b : 128 * b + 128].reshape(SLAB_LON, CIN, 128) for b in range(4)], 1
            )
            fx[1 + s * SLAB_LON : 1 + s * SLAB_LON + SLAB_LON, :, half * 128 : half * 128 + 128] = wide.astype(BF16)

    for step in range(8):
        load_slab(step)
    fx[0, :, 0:128] = fx[64, :, 128:256]
    fx[0, :, 128:256] = fx[64, :, 0:128]
    fx[65, :, 0:128] = fx[1, :, 128:256]
    fx[65, :, 128:256] = fx[1, :, 0:128]

    def stem(g):
        n = STEM_GROUP
        window = fx[pl.ds(2 * n * g, 2 * n + 2)].reshape((2 * n + 2) * 96, 256)
        pre = dot(w1_ref[...], window)
        stem_pre[n * g : n * g + n] = pre.reshape(n, C1, 256)
        act = (pre * sigmoid(pre)).astype(BF16)
        taps = dot(act, staps_ref[...])
        wide = jnp.concatenate([taps[:, 128 * b : 128 * b + 128].reshape(n, C1, 128) for b in range(3)], 1)
        mx[1 + n * g : 1 + n * g + n] = wide.astype(BF16)

    for step in range(32 // STEM_GROUP):
        stem(step)
    mx[0] = swapped(mx[32])
    mx[33] = jnp.zeros((96, 128), BF16)

    def mid(g):
        n = MID_GROUP
        window = mx[pl.ds(2 * n * g, 2 * n + 1)].reshape((2 * n + 1) * 96, 128)
        pre = dot(w2_ref[...], window)
        mid_pre[n * g : n * g + n] = pre.reshape(n, C2, 128)
        act = pre * sigmoid(pre)
        for k in range(n):
            one = act[k * C2 : k * C2 + C2]
            hx[n * g + k + 1] = jnp.concatenate([earlier(one), one, later(one)], 0).astype(BF16)

    for step in range(16 // MID_GROUP):
        mid(step)
    hx[0] = swapped(hx[16])
    hx[17] = swapped(hx[1])

    for edge in (0, 1, 18, 19):
        hc_pad[edge] = jnp.zeros((C2, 128), BF16)
    out_w = jnp.broadcast_to(ow_ref[...], (C2, 128))

    def head(g, out_sum):
        n = HEAD_GROUP
        window = hx[pl.ds(n * g, n + 2)].reshape((n + 2) * 192, 128)
        pre = dot(w3_ref[...], window)
        sigma = sigmoid(pre)
        act = (pre * sigma).astype(BF16).astype(F32)
        bend = sigma * (1.0 + pre * (1.0 - sigma))
        for k in range(n):
            r = n * g + k
            here = slice(k * C2, k * C2 + C2)
            cot = jnp.broadcast_to(pc_ref[r : r + 1, :], (C2, 128))
            pred_ref[r : r + 1, :] = jnp.sum(out_w * act[here], 0, keepdims=True)
            out_sum = out_sum + cot * act[here]
            hc = (cot * out_w) * bend[here]
            hc_pad[r + 2] = hc.astype(BF16)
            hc_wide[r + 1] = jnp.concatenate([earlier(hc), hc, later(hc)], 0).astype(BF16)
        return out_sum

    out_sum = jnp.zeros((C2, 128), F32)
    for step in range(16 // HEAD_GROUP):
        out_sum = head(step, out_sum)
    sums_ref[576:640, :] = out_sum
    hc_wide[0] = swapped(hc_wide[16])
    hc_wide[17] = swapped(hc_wide[1])

    for edge in (0, 17):
        mc_pad[edge] = jnp.zeros((C2, 128), BF16)

    def head_back(g):
        n = HEAD_GROUP
        window = hc_wide[pl.ds(n * g, n + 2)].reshape((n + 2) * 192, 128)
        grad = dot(w3b_ref[...], window).astype(BF16).astype(F32)
        mc = grad * slope_of(mid_pre[n * g : n * g + n].reshape(n * C2, 128))
        for k in range(n):
            one = mc[k * C2 : k * C2 + C2]
            mc_pad[n * g + k + 1] = one.astype(BF16)
            mc_pair[n * g + k] = jnp.concatenate([one, later(one)], 0).astype(BF16)

    for step in range(16 // HEAD_GROUP):
        head_back(step)
    mc_pair[16] = swapped(mc_pair[0])

    for edge in (0, 33):
        sc_pad[edge] = jnp.zeros((C1, 256), BF16)

    def mid_back(m):
        parts = []
        for k in range(2):
            window = mc_pair[2 * m + k : 2 * m + k + 2].reshape(256, 128)
            grad = dot(w2b_ref[...], window).astype(BF16)
            parts.append(jnp.concatenate([grad[0:64], grad[64:128]], 1))
        grad = dot(jnp.concatenate(parts, 0), inter_ref[...])
        cot = (grad * slope_of(stem_pre[4 * m : 4 * m + 4].reshape(128, 256))).astype(BF16)
        sc_pad[4 * m + 1 : 4 * m + 1 + 4] = cot.reshape(4, C1, 256)
        out = dot(rows_ref[...], cot).astype(BF16)
        wire_ref[m, SUM_ROWS:WIRE_ROWS] = out[:, 0:128]
        wire_ref[m + 8, SUM_ROWS:WIRE_ROWS] = out[:, 128:256]

    for step in range(8):
        mid_back(step)

    def head_sum(p, total):
        left = jnp.concatenate([hc_pad[2 * p + k : 2 * p + k + 3].reshape(192, 128) for k in range(2)], 1)
        right = jnp.concatenate([hx[2 * p], hx[2 * p + 1]], 1)
        return total + dot_t(left, right)

    total = jnp.zeros((192, 192), F32)
    for step in range(9):
        total = head_sum(step, total)
    sums_ref[0:192, :] = total[:, 0:128]
    sums_ref[192:384, 0:64] = total[:, 128:192]

    def mid_sum(m, total):
        return total + dot_t(mx[2 * m : 2 * m + 2].reshape(192, 128), mc_pad[m : m + 2].reshape(128, 128))

    total = jnp.zeros((192, 128), F32)
    for step in range(17):
        total = mid_sum(step, total)
    sums_ref[384:576, :] = total

    def stem_sum(m, total):
        return total + dot_t(fx[2 * m : 2 * m + 2].reshape(192, 256), sc_pad[m : m + 2].reshape(64, 256))

    total = jnp.zeros((192, 64), F32)
    for step in range(33):
        total = stem_sum(step, total)
    sums_ref[192:384, 64:128] = total

    for s in range(SLABS):
        term = sums_ref[s * SHARE : s * SHARE + SHARE, :]
        near = term.astype(BF16).astype(F32)
        wire_ref[s, 0:SUM_ROWS] = jnp.concatenate([near, term - near], 0).astype(BF16)


def scenario_pass(x, weights, out_weight, cotangent):
    out_shape = (
        jax.ShapeDtypeStruct((16, 128), F32),
        jax.ShapeDtypeStruct((SLABS, WIRE_ROWS, 128), BF16),
    )
    scratch = [
        pltpu.VMEM((SLABS * SHARE, 128), F32),
        pltpu.VMEM((66, 96, 256), BF16),
        pltpu.VMEM((32, C1, 256), F32),
        pltpu.VMEM((34, 96, 128), BF16),
        pltpu.VMEM((16, C2, 128), F32),
        pltpu.VMEM((18, 192, 128), BF16),
        pltpu.VMEM((18, 192, 128), BF16),
        pltpu.VMEM((20, C2, 128), BF16),
        pltpu.VMEM((17, 128, 128), BF16),
        pltpu.VMEM((18, C2, 128), BF16),
        pltpu.VMEM((34, C1, 256), BF16),
    ]
    whole = pl.BlockSpec(memory_space=pltpu.VMEM)
    return pl.pallas_call(
        scenario_kernel,
        out_shape=out_shape,
        in_specs=[whole] * 13,
        out_specs=(whole,) * 2,
        scratch_shapes=scratch,
        compiler_params=pltpu.CompilerParams(vmem_limit_bytes=48 << 20),
        cost_estimate=pl.CostEstimate(flops=4 * 10**9, bytes_accessed=4 << 20, transcendentals=10**6),
        name="scenario",
    )(x, *weights, *selections(), out_weight.reshape(C2, 1), cotangent)


def exchanged(value, axis):
    return lax.all_to_all(value, axis, split_axis=0, concat_axis=0, tiled=True)


def lon_share_kernel(got_ref, out_ref):
    total = jnp.zeros((SUM_ROWS, 128), F32)
    for k in range(SLABS):
        total = total + got_ref[k].astype(F32)
    share = (total[0:SHARE] + total[SHARE:SUM_ROWS]).astype(BF16)
    for k in range(SLABS):
        out_ref[k] = share


def rep_share_kernel(got_ref, out_ref):
    total = jnp.zeros((SHARE, 128), F32)
    for k in range(SLABS):
        total = total + got_ref[k].astype(F32)
    share = total.astype(BF16)
    for k in range(SLABS):
        out_ref[k] = share


def unpack_kernel(factor, sums_ref, stem_ref, mid_ref, head_ref, out_ref, wide):
    wide[...] = sums_ref[...].astype(F32) * factor
    for a in range(3):
        at = (2 - a) * C2
        head_ref[a, 0] = wide[at : at + C2, 0:64]
        head_ref[a, 1] = wide[at : at + C2, 64:128]
        head_ref[a, 2] = wide[192 + at : 192 + at + C2, 0:64]
        lanes = slice(0, 64) if a == 2 else slice(64, 128)
        for b in range(3):
            at = 384 + a % 2 * 96 + b * C1
            mid_ref[a, b] = wide[at : at + C1, lanes]
    for a in range(4):
        lanes = slice(64, 96) if a >= 2 else slice(96, 128)
        for c in range(CIN):
            rows = wide[pl.ds(192 + a % 2 * 96 + c, 4, stride=CIN), :]
            stem_ref[c, a] = rows[:, lanes]
    ones = jnp.full((8, 128), 1.0, BF16)
    out_ref[...] = dot_t(ones, sums_ref[576:640])[0:1] * factor


def on_chip(kernel, outs, scratch=(), name=None):
    whole = pl.BlockSpec(memory_space=pltpu.VMEM)
    single = not isinstance(outs, tuple)
    return lambda *args: pl.pallas_call(
        kernel,
        out_shape=outs,
        in_specs=[whole] * len(args),
        out_specs=whole if single else (whole,) * len(outs),
        scratch_shapes=scratch,
        name=name,
    )(*args)


def summed_everywhere(got, factor):
    shares = jax.ShapeDtypeStruct((SLABS, SHARE, 128), BF16)
    share = pl.pallas_call(
        lon_share_kernel,
        grid=(1,),
        out_shape=shares,
        in_specs=[pl.BlockSpec((SLABS, SUM_ROWS, 128), lambda i: (0, 0, 0))],
        out_specs=pl.BlockSpec((SLABS, SHARE, 128), lambda i: (0, 0, 0)),
        name="lon_share",
    )(got)
    share = on_chip(rep_share_kernel, shares, name="rep_share")(exchanged(share, "rep"))
    sums = exchanged(share, "lon").reshape(SLABS * SHARE, 128)
    outs = (
        jax.ShapeDtypeStruct((CIN, 4, 4, C1), F32),
        jax.ShapeDtypeStruct((3, 3, C1, C2), F32),
        jax.ShapeDtypeStruct((3, 3, C2, C2), F32),
        jax.ShapeDtypeStruct((1, C2), F32),
    )
    scratch = [pltpu.VMEM((SLABS * SHARE, 128), F32)]
    stem, mid, head, out = on_chip(functools.partial(unpack_kernel, factor), outs, scratch, "unpack")(sums)
    return stem.transpose(3, 0, 1, 2), mid.transpose(3, 2, 0, 1), head.transpose(2, 3, 0, 1), out.reshape(C2)


def local(fields, stem_weight, mid_weight, head_weight, out_weight, pred_cotangent):
    x = exchanged(fields.reshape(SLABS, CIN * SLAB_LON, LAT), "lon")
    weights = kernel_weights(stem_weight, mid_weight, head_weight)
    cotangent = pred_cotangent.reshape(2, 16, 64).transpose(1, 0, 2).reshape(16, 128)
    prediction, wire = scenario_pass(x, weights, out_weight, cotangent)
    prediction = prediction.reshape(16, 2, 64).transpose(1, 0, 2).reshape(1, 32, 64)
    got = exchanged(wire, "lon")
    stem_cotangent = got[:, SUM_ROWS:].reshape(SLABS, C1, 4, 128)
    factor = 1.0 / (fields.shape[0] * lax.axis_size("rep"))
    return (prediction, stem_cotangent, *summed_everywhere(got, factor))


def solution(mesh):
    placed = (P("rep", None, "lon", None), P(), P(), P(), P(), P(("rep", "lon"), None, None))
    return jax.shard_map(
        local,
        mesh=mesh,
        in_specs=placed,
        out_specs=(P(("rep", "lon"), None, None), P("rep", None, "lon", None), P(), P(), P(), P()),
        check_vma=False,
    )
```

```python
import functools

import jax
import jax.numpy as jnp
from jax import lax
from jax.experimental import pallas as pl
from jax.experimental.pallas import tpu as pltpu
from jax.sharding import PartitionSpec as P

BF16, F32 = jnp.bfloat16, jnp.float32
SLABS, CIN, SLAB_LON, LAT = 16, 24, 8, 256
C1, C2 = 32, 64
COT_ROWS, SHARE = 128, 40
WIRE_ROWS = SHARE + COT_ROWS
STEM_GROUP, STEM_BATCH, MID_GROUP, HEAD_GROUP = 4, 4, 2, 2
SLAB_BATCH, BACK_BATCH = 2, 8


def one_hot(shape, test):
    rows = lax.broadcasted_iota(jnp.int32, shape, 0)
    cols = lax.broadcasted_iota(jnp.int32, shape, 1)
    return jnp.where(test(rows, cols), 1.0, 0.0).astype(BF16)


def selections():
    regroup = one_hot(
        (CIN * SLAB_LON, CIN * SLAB_LON),
        lambda r, c: (r % CIN == c // SLAB_LON) & (r // CIN == c % SLAB_LON),
    )
    field_taps = one_hot((LAT, 512), lambda r, c: r == 2 * (c % 128) + c // 128 - 1)
    stem_taps = one_hot(
        (256, 384),
        lambda r, c: (r // 128 == c % 128 // 64) & (r % 128 == 2 * (c % 64) + c // 128 - 1),
    )
    interleave = one_hot(
        (256, 256),
        lambda r, c: (r % 128 // 64 == c // 128) & (c % 128 == 2 * (r % 64) + r // 128),
    )
    return regroup, field_taps, stem_taps, interleave


def toeplitz(rows, group, step):
    out, window, depth = rows.shape
    width = step * (group - 1) + window
    copies = [
        jnp.pad(rows, ((0, 0), (step * at, width - window - step * at), (0, 0))) for at in range(group)
    ]
    return jnp.stack(copies).reshape(group * out, width * depth)


def kernel_weights(stem_weight, mid_weight, head_weight):
    stem = stem_weight.transpose(0, 2, 3, 1).reshape(C1, 4, 4 * CIN)
    mid = mid_weight.transpose(0, 2, 3, 1).reshape(C2, 3, 3 * C1)
    head = head_weight.transpose(0, 2, 3, 1).reshape(C2, 3, 3 * C2)
    head_back = head_weight[:, :, ::-1, ::-1].transpose(1, 2, 3, 0).reshape(C2, 3, 3 * C2)
    none = jnp.zeros((C1, C2), mid_weight.dtype)
    blocks = []
    for lat_odd in (0, 1):
        for lon_odd in (0, 1):
            row = []
            for next_lon in (0, 1):
                for next_lat in (0, 1):
                    if next_lon > lon_odd or next_lat > lat_odd:
                        row.append(none)
                    else:
                        a = 1 if not lon_odd else 2 - 2 * next_lon
                        b = 1 if not lat_odd else 2 - 2 * next_lat
                        row.append(mid_weight[:, :, a, b].T)
            blocks.append(jnp.concatenate(row, 1))
    mid_back = jnp.concatenate(blocks, 0)
    return (
        toeplitz(stem, STEM_GROUP, 2),
        toeplitz(mid, MID_GROUP, 2),
        toeplitz(head, HEAD_GROUP, 1),
        toeplitz(head_back, HEAD_GROUP, 1),
        mid_back,
    )


def dot(left, right):
    return jnp.dot(left, right, preferred_element_type=F32)


def dot_t(left, right):
    return lax.dot_general(left, right, (((1,), (1,)), ((), ())), preferred_element_type=F32)


def swapped(block):
    return pltpu.roll(block.astype(F32), 64, 1).astype(BF16)


def sigmoid(values):
    return 1.0 / (1.0 + jnp.exp(-values))


def slope_of(values):
    sigma = sigmoid(values)
    return sigma * (1.0 + values * (1.0 - sigma))


def scenario_kernel(
    x_ref, w1_ref, w2_ref, w3_ref, w3b_ref, w2b_ref, regroup_ref, ftaps_ref, staps_ref, inter_ref,
    ow_ref, pc_ref,
    pred_ref, wire_ref,
    sums_ref, fx, stem_pre, mx, mid_pre, hx, hc_wide, hc_pad, mc_pair, mc_pad, sc_pad,
):
    lane = lax.broadcasted_iota(jnp.int32, (C2, 128), 1) % 64
    first, last = lane == 0, lane == 63

    def earlier(block):
        return jnp.where(first, 0.0, pltpu.roll(block, 1, 1))

    def later(block):
        return jnp.where(last, 0.0, pltpu.roll(block, 127, 1))

    def load_slabs(at):
        places = [(s, half) for s in range(at, at + SLAB_BATCH) for half in (0, 1)]
        parts = [dot(regroup_ref[...], x_ref[s + 8 * half]).astype(BF16) for s, half in places]
        all_taps = dot(jnp.concatenate(parts, 0), ftaps_ref[...])
        for k, (s, half) in enumerate(places):
            taps = all_taps[192 * k : 192 * k + 192]
            wide = jnp.concatenate(
                [taps[:, 128 * b : 128 * b + 128].reshape(SLAB_LON, CIN, 128) for b in range(4)], 1
            )
            rows = slice(1 + s * SLAB_LON, 1 + s * SLAB_LON + SLAB_LON)
            fx[rows, :, half * 128 : half * 128 + 128] = wide.astype(BF16)

    for at in range(0, 8, SLAB_BATCH):
        load_slabs(at)
    fx[0, :, 0:128] = fx[64, :, 128:256]
    fx[0, :, 128:256] = fx[64, :, 0:128]
    fx[65, :, 0:128] = fx[1, :, 128:256]
    fx[65, :, 128:256] = fx[1, :, 0:128]

    def stem(g):
        n = STEM_GROUP
        window = fx[pl.ds(2 * n * g, 2 * n + 2)].reshape((2 * n + 2) * 96, 256)
        pre = dot(w1_ref[...], window)
        stem_pre[n * g : n * g + n] = pre.reshape(n, C1, 256)
        return (pre * sigmoid(pre)).astype(BF16)

    def stem_taps(acts, at):
        n = STEM_GROUP * len(acts)
        taps = dot(jnp.concatenate(acts, 0), staps_ref[...])
        wide = jnp.concatenate([taps[:, 128 * b : 128 * b + 128].reshape(n, C1, 128) for b in range(3)], 1)
        mx[1 + at : 1 + at + n] = wide.astype(BF16)

    for at in range(0, 32 // STEM_GROUP, STEM_BATCH):
        stem_taps([stem(at + k) for k in range(STEM_BATCH)], at * STEM_GROUP)
    mx[0] = swapped(mx[32])
    mx[33] = jnp.zeros((96, 128), BF16)

    def mid(g):
        n = MID_GROUP
        window = mx[pl.ds(2 * n * g, 2 * n + 1)].reshape((2 * n + 1) * 96, 128)
        pre = dot(w2_ref[...], window)
        mid_pre[n * g : n * g + n] = pre.reshape(n, C2, 128)
        act = pre * sigmoid(pre)
        for k in range(n):
            one = act[k * C2 : k * C2 + C2]
            hx[n * g + k + 1] = jnp.concatenate([earlier(one), one, later(one)], 0).astype(BF16)

    for step in range(16 // MID_GROUP):
        mid(step)
    hx[0] = swapped(hx[16])
    hx[17] = swapped(hx[1])

    for edge in (0, 1, 18, 19):
        hc_pad[edge] = jnp.zeros((C2, 128), BF16)
    out_w = jnp.broadcast_to(ow_ref[...], (C2, 128))

    def head(g, out_sum):
        n = HEAD_GROUP
        window = hx[pl.ds(n * g, n + 2)].reshape((n + 2) * 192, 128)
        pre = dot(w3_ref[...], window)
        sigma = sigmoid(pre)
        act = (pre * sigma).astype(BF16).astype(F32)
        bend = sigma * (1.0 + pre * (1.0 - sigma))
        for k in range(n):
            r = n * g + k
            here = slice(k * C2, k * C2 + C2)
            cot = jnp.broadcast_to(pc_ref[r : r + 1, :], (C2, 128))
            pred_ref[r : r + 1, :] = jnp.sum(out_w * act[here], 0, keepdims=True)
            out_sum = out_sum + cot * act[here]
            hc = (cot * out_w) * bend[here]
            hc_pad[r + 2] = hc.astype(BF16)
            hc_wide[r + 1] = jnp.concatenate([earlier(hc), hc, later(hc)], 0).astype(BF16)
        return out_sum

    out_sum = jnp.zeros((C2, 128), F32)
    for step in range(16 // HEAD_GROUP):
        out_sum = head(step, out_sum)
    sums_ref[576:640, :] = out_sum
    hc_wide[0] = swapped(hc_wide[16])
    hc_wide[17] = swapped(hc_wide[1])

    for edge in (0, 17):
        mc_pad[edge] = jnp.zeros((C2, 128), BF16)

    def head_back(g):
        n = HEAD_GROUP
        window = hc_wide[pl.ds(n * g, n + 2)].reshape((n + 2) * 192, 128)
        grad = dot(w3b_ref[...], window).astype(BF16).astype(F32)
        mc = grad * slope_of(mid_pre[n * g : n * g + n].reshape(n * C2, 128))
        for k in range(n):
            one = mc[k * C2 : k * C2 + C2]
            mc_pad[n * g + k + 1] = one.astype(BF16)
            mc_pair[n * g + k] = jnp.concatenate([one, later(one)], 0).astype(BF16)

    for step in range(16 // HEAD_GROUP):
        head_back(step)
    mc_pair[16] = swapped(mc_pair[0])

    for edge in (0, 33):
        sc_pad[edge] = jnp.zeros((C1, 256), BF16)

    def mid_back(at):
        parts = []
        for r in range(at, at + BACK_BATCH):
            window = mc_pair[r : r + 2].reshape(256, 128)
            grad = dot(w2b_ref[...], window).astype(BF16)
            parts.append(jnp.concatenate([grad[0:64], grad[64:128]], 1))
        grads = dot(jnp.concatenate(parts, 0), inter_ref[...])
        for m in range(at // 2, (at + BACK_BATCH) // 2):
            grad = grads[128 * m - 64 * at : 128 * m - 64 * at + 128]
            cot = (grad * slope_of(stem_pre[4 * m : 4 * m + 4].reshape(128, 256))).astype(BF16)
            sc_pad[4 * m + 1 : 4 * m + 5] = cot.reshape(4, C1, 256)
            wire_ref[m, SHARE:WIRE_ROWS] = cot[:, 0:128]
            wire_ref[m + 8, SHARE:WIRE_ROWS] = cot[:, 128:256]

    for at in range(0, 16, BACK_BATCH):
        mid_back(at)

    def head_sum(p, total):
        left = jnp.concatenate([hc_pad[2 * p + k : 2 * p + k + 3].reshape(192, 128) for k in range(2)], 1)
        right = jnp.concatenate([hx[2 * p], hx[2 * p + 1]], 1)
        return total + dot_t(left, right)

    total = jnp.zeros((192, 192), F32)
    for step in range(9):
        total = head_sum(step, total)
    sums_ref[0:192, :] = total[:, 0:128]
    sums_ref[192:384, 0:64] = total[:, 128:192]

    def mid_sum(m, total):
        return total + dot_t(mx[2 * m : 2 * m + 2].reshape(192, 128), mc_pad[m : m + 2].reshape(128, 128))

    total = jnp.zeros((192, 128), F32)
    for step in range(17):
        total = mid_sum(step, total)
    sums_ref[384:576, :] = total

    def stem_sum(m, total):
        return total + dot_t(fx[2 * m : 2 * m + 2].reshape(192, 256), sc_pad[m : m + 2].reshape(64, 256))

    total = jnp.zeros((192, 64), F32)
    for step in range(33):
        total = stem_sum(step, total)
    sums_ref[192:384, 64:128] = total

    for s in range(SLABS):
        wire_ref[s, 0:SHARE] = sums_ref[s * SHARE : s * SHARE + SHARE, :].astype(BF16)


def scenario_pass(x, weights, out_weight, cotangent):
    out_shape = (
        jax.ShapeDtypeStruct((16, 128), F32),
        jax.ShapeDtypeStruct((SLABS, WIRE_ROWS, 128), BF16),
    )
    scratch = [
        pltpu.VMEM((SLABS * SHARE, 128), F32),
        pltpu.VMEM((66, 96, 256), BF16),
        pltpu.VMEM((32, C1, 256), F32),
        pltpu.VMEM((34, 96, 128), BF16),
        pltpu.VMEM((16, C2, 128), F32),
        pltpu.VMEM((18, 192, 128), BF16),
        pltpu.VMEM((18, 192, 128), BF16),
        pltpu.VMEM((20, C2, 128), BF16),
        pltpu.VMEM((17, 128, 128), BF16),
        pltpu.VMEM((18, C2, 128), BF16),
        pltpu.VMEM((34, C1, 256), BF16),
    ]
    whole = pl.BlockSpec(memory_space=pltpu.VMEM)
    return pl.pallas_call(
        scenario_kernel,
        out_shape=out_shape,
        in_specs=[whole] * 12,
        out_specs=(whole,) * 2,
        scratch_shapes=scratch,
        compiler_params=pltpu.CompilerParams(vmem_limit_bytes=32 << 20),
        cost_estimate=pl.CostEstimate(flops=4 * 10**9, bytes_accessed=4 << 20, transcendentals=10**6),
        name="scenario",
    )(x, *weights, *selections(), out_weight.reshape(C2, 1), cotangent)


def exchanged(value, axis):
    return lax.all_to_all(value, axis, split_axis=0, concat_axis=0, tiled=True)


def share_kernel(got_ref, out_ref):
    total = jnp.zeros((SHARE, 128), F32)
    for k in range(SLABS):
        total = total + got_ref[k, 0:SHARE].astype(F32)
    share = total.astype(BF16)
    for k in range(SLABS):
        out_ref[k] = share


def unpack_kernel(factor, sums_ref, stem_ref, mid_ref, head_ref, out_ref, wide):
    wide[...] = sums_ref[...].astype(F32) * factor
    for a in range(3):
        at = (2 - a) * C2
        head_ref[a, 0] = wide[at : at + C2, 0:64]
        head_ref[a, 1] = wide[at : at + C2, 64:128]
        head_ref[a, 2] = wide[192 + at : 192 + at + C2, 0:64]
        lanes = slice(0, 64) if a == 2 else slice(64, 128)
        for b in range(3):
            at = 384 + a % 2 * 96 + b * C1
            mid_ref[a, b] = wide[at : at + C1, lanes]
    for a in range(4):
        lanes = slice(64, 96) if a >= 2 else slice(96, 128)
        for c in range(CIN):
            rows = wide[pl.ds(192 + a % 2 * 96 + c, 4, stride=CIN), :]
            stem_ref[c, a] = rows[:, lanes]
    ones = jnp.full((8, 128), 1.0, BF16)
    out_ref[...] = dot_t(ones, sums_ref[576:640])[0:1] * factor


def on_chip(kernel, outs, scratch=(), name=None):
    whole = pl.BlockSpec(memory_space=pltpu.VMEM)
    single = not isinstance(outs, tuple)
    return lambda *args: pl.pallas_call(
        kernel,
        out_shape=outs,
        in_specs=[whole] * len(args),
        out_specs=whole if single else (whole,) * len(outs),
        scratch_shapes=scratch,
        compiler_params=pltpu.CompilerParams(vmem_limit_bytes=8 << 20),
        name=name,
    )(*args)


def summed_everywhere(got, factor):
    shares = jax.ShapeDtypeStruct((SLABS, SHARE, 128), BF16)
    share = on_chip(share_kernel, shares, name="lon_share")(got)
    share = on_chip(share_kernel, shares, name="rep_share")(exchanged(share, "rep"))
    sums = exchanged(share, "lon").reshape(SLABS * SHARE, 128)
    outs = (
        jax.ShapeDtypeStruct((CIN, 4, 4, C1), F32),
        jax.ShapeDtypeStruct((3, 3, C1, C2), F32),
        jax.ShapeDtypeStruct((3, 3, C2, C2), F32),
        jax.ShapeDtypeStruct((1, C2), F32),
    )
    scratch = [pltpu.VMEM((SLABS * SHARE, 128), F32)]
    stem, mid, head, out = on_chip(functools.partial(unpack_kernel, factor), outs, scratch, "unpack")(sums)
    return stem.transpose(3, 0, 1, 2), mid.transpose(3, 2, 0, 1), head.transpose(2, 3, 0, 1), out.reshape(C2)


def local(fields, stem_weight, mid_weight, head_weight, out_weight, pred_cotangent):
    x = exchanged(fields.reshape(SLABS, CIN * SLAB_LON, LAT), "lon")
    weights = kernel_weights(stem_weight, mid_weight, head_weight)
    cotangent = pred_cotangent.reshape(2, 16, 64).transpose(1, 0, 2).reshape(16, 128)
    prediction, wire = scenario_pass(x, weights, out_weight, cotangent)
    prediction = prediction.reshape(16, 2, 64).transpose(1, 0, 2).reshape(1, 32, 64)
    got = exchanged(wire, "lon")
    stem_cotangent = got[:, SHARE:].reshape(SLABS, 4, C1, 128).transpose(0, 2, 1, 3)
    factor = 1.0 / (fields.shape[0] * lax.axis_size("rep"))
    return (prediction, stem_cotangent, *summed_everywhere(got, factor))


def solution(mesh):
    placed = (P("rep", None, "lon", None), P(), P(), P(), P(), P(("rep", "lon"), None, None))
    return jax.shard_map(
        local,
        mesh=mesh,
        in_specs=placed,
        out_specs=(P(("rep", "lon"), None, None), P("rep", None, "lon", None), P(), P(), P(), P()),
        check_vma=False,
    )
```

```python
import functools

import jax
import jax.numpy as jnp
from jax import lax
from jax.experimental import pallas as pl
from jax.experimental.pallas import tpu as pltpu
from jax.sharding import PartitionSpec as P

BF16, F32 = jnp.bfloat16, jnp.float32
SLABS, CIN, SLAB_LON, LAT = 16, 24, 8, 256
C1, C2 = 32, 64
COT_ROWS, SHARE = 128, 40
WIRE_ROWS = SHARE + COT_ROWS
STEM_GROUP, STEM_BATCH, MID_GROUP, HEAD_GROUP = 4, 4, 2, 2
SLAB_BATCH, BACK_BATCH = 2, 8


def one_hot(shape, test):
    rows = lax.broadcasted_iota(jnp.int32, shape, 0)
    cols = lax.broadcasted_iota(jnp.int32, shape, 1)
    return jnp.where(test(rows, cols), 1.0, 0.0).astype(BF16)


def selections():
    regroup = one_hot(
        (CIN * SLAB_LON, CIN * SLAB_LON),
        lambda r, c: (r % CIN == c // SLAB_LON) & (r // CIN == c % SLAB_LON),
    )
    field_taps = one_hot((LAT, 256), lambda r, c: r == 2 * (c % 128) + c // 128)
    stem_taps = one_hot(
        (256, 256),
        lambda r, c: (r // 128 == c % 128 // 64) & (r % 128 == 2 * (c % 64) + c // 128),
    )
    interleave = one_hot(
        (256, 256),
        lambda r, c: (r % 128 // 64 == c // 128) & (c % 128 == 2 * (r % 64) + r // 128),
    )
    return regroup, field_taps, stem_taps, interleave


def toeplitz(rows, group, step):
    out, window, depth = rows.shape
    width = step * (group - 1) + window
    copies = [
        jnp.pad(rows, ((0, 0), (step * at, width - window - step * at), (0, 0))) for at in range(group)
    ]
    return jnp.stack(copies).reshape(group * out, width * depth)


def kernel_weights(stem_weight, mid_weight, head_weight):
    stem = stem_weight.transpose(0, 2, 3, 1).reshape(C1, 4, 4 * CIN)
    mid = mid_weight.transpose(0, 2, 3, 1).reshape(C2, 3, 3 * C1)
    head = head_weight.transpose(0, 2, 3, 1).reshape(C2, 3, 3 * C2)
    head_back = head_weight[:, :, ::-1, ::-1].transpose(1, 2, 3, 0).reshape(C2, 3, 3 * C2)
    none = jnp.zeros((C1, C2), mid_weight.dtype)
    blocks = []
    for lat_odd in (0, 1):
        for lon_odd in (0, 1):
            row = []
            for next_lon in (0, 1):
                for next_lat in (0, 1):
                    if next_lon > lon_odd or next_lat > lat_odd:
                        row.append(none)
                    else:
                        a = 1 if not lon_odd else 2 - 2 * next_lon
                        b = 1 if not lat_odd else 2 - 2 * next_lat
                        row.append(mid_weight[:, :, a, b].T)
            blocks.append(jnp.concatenate(row, 1))
    mid_back = jnp.concatenate(blocks, 0)
    return (
        toeplitz(stem, STEM_GROUP, 2),
        toeplitz(mid, MID_GROUP, 2),
        toeplitz(head, HEAD_GROUP, 1),
        toeplitz(head_back, HEAD_GROUP, 1),
        mid_back,
    )


def dot(left, right):
    return jnp.dot(left, right, preferred_element_type=F32)


def dot_t(left, right):
    return lax.dot_general(left, right, (((1,), (1,)), ((), ())), preferred_element_type=F32)


def turned(block):
    return block.astype(F32).T.astype(BF16)


def swapped(block):
    return pltpu.roll(block.astype(F32), 64, 1).astype(BF16)


def sigmoid(values):
    return 1.0 / (1.0 + jnp.exp(-values))


def slope_of(values):
    sigma = sigmoid(values)
    return sigma * (1.0 + values * (1.0 - sigma))


def scenario_kernel(
    x_ref, w1_ref, w2_ref, w3_ref, w3b_ref, w2b_ref, regroup_ref, ftaps_ref, staps_ref, inter_ref,
    ow_ref, pc_ref,
    pred_ref, wire_ref,
    sums_ref, fx, stem_pre, mx, mid_pre, hx, hc_wide, hc_pad, mc_pair, mc_pad, sc_pad,
):
    lane = lax.broadcasted_iota(jnp.int32, (C2, 128), 1) % 64
    first, last = lane == 0, lane == 63

    def earlier(block):
        return jnp.where(first, 0.0, pltpu.roll(block, 1, 1))

    def later(block):
        return jnp.where(last, 0.0, pltpu.roll(block, 127, 1))

    lat = lax.broadcasted_iota(jnp.int32, (192, 128), 1)

    def load_slabs(at):
        places = [(s, half) for s in range(at, at + SLAB_BATCH) for half in (0, 1)]
        parts = [dot(regroup_ref[...], x_ref[s + 8 * half]).astype(BF16) for s, half in places]
        all_taps = dot(jnp.concatenate(parts, 0), ftaps_ref[...])
        for k, (s, half) in enumerate(places):
            taps = all_taps[192 * k : 192 * k + 192]
            even, odd = taps[:, 0:128], taps[:, 128:256]
            before = jnp.where(lat == 0, 0.0, pltpu.roll(odd, 1, 1))
            after = jnp.where(lat == 127, 0.0, pltpu.roll(even, 127, 1))
            wide = jnp.concatenate([t.reshape(SLAB_LON, CIN, 128) for t in (before, even, odd, after)], 1)
            rows = slice(1 + s * SLAB_LON, 1 + s * SLAB_LON + SLAB_LON)
            fx[rows, :, half * 128 : half * 128 + 128] = wide.astype(BF16)

    for at in range(0, 8, SLAB_BATCH):
        load_slabs(at)
    fx[0, :, 0:128] = fx[64, :, 128:256]
    fx[0, :, 128:256] = fx[64, :, 0:128]
    fx[65, :, 0:128] = fx[1, :, 128:256]
    fx[65, :, 128:256] = fx[1, :, 0:128]

    def stem(g):
        n = STEM_GROUP
        window = fx[pl.ds(2 * n * g, 2 * n + 2)].reshape((2 * n + 2) * 96, 256)
        pre = dot(w1_ref[...], window)
        stem_pre[n * g : n * g + n] = pre.reshape(n, C1, 256)
        return (pre * sigmoid(pre)).astype(BF16)

    def stem_taps(acts, at):
        n = STEM_GROUP * len(acts)
        taps = dot(jnp.concatenate(acts, 0), staps_ref[...])
        even, odd = taps[:, 0:128], taps[:, 128:256]
        lat = lax.broadcasted_iota(jnp.int32, odd.shape, 1) % 64
        before = jnp.where(lat == 0, 0.0, pltpu.roll(odd, 1, 1))
        wide = jnp.concatenate([t.reshape(n, C1, 128) for t in (before, even, odd)], 1)
        mx[1 + at : 1 + at + n] = wide.astype(BF16)

    for at in range(0, 32 // STEM_GROUP, STEM_BATCH):
        stem_taps([stem(at + k) for k in range(STEM_BATCH)], at * STEM_GROUP)
    mx[0] = swapped(mx[32])
    mx[33] = jnp.zeros((96, 128), BF16)

    def mid(g):
        n = MID_GROUP
        window = mx[pl.ds(2 * n * g, 2 * n + 1)].reshape((2 * n + 1) * 96, 128)
        pre = dot(w2_ref[...], window)
        mid_pre[n * g : n * g + n] = pre.reshape(n, C2, 128)
        act = pre * sigmoid(pre)
        for k in range(n):
            one = act[k * C2 : k * C2 + C2]
            hx[n * g + k + 1] = jnp.concatenate([earlier(one), one, later(one)], 0).astype(BF16)

    for step in range(16 // MID_GROUP):
        mid(step)
    hx[0] = swapped(hx[16])
    hx[17] = swapped(hx[1])

    for edge in (0, 1, 18, 19):
        hc_pad[edge] = jnp.zeros((C2, 128), BF16)
    out_w = jnp.broadcast_to(ow_ref[...], (C2, 128))

    def head(g, out_sum):
        n = HEAD_GROUP
        window = hx[pl.ds(n * g, n + 2)].reshape((n + 2) * 192, 128)
        pre = dot(w3_ref[...], window)
        sigma = sigmoid(pre)
        act = (pre * sigma).astype(BF16).astype(F32)
        bend = sigma * (1.0 + pre * (1.0 - sigma))
        for k in range(n):
            r = n * g + k
            here = slice(k * C2, k * C2 + C2)
            cot = jnp.broadcast_to(pc_ref[r : r + 1, :], (C2, 128))
            pred_ref[r : r + 1, :] = jnp.sum(out_w * act[here], 0, keepdims=True)
            out_sum = out_sum + cot * act[here]
            hc = (cot * out_w) * bend[here]
            hc_pad[r + 2] = hc.astype(BF16)
            hc_wide[r + 1] = jnp.concatenate([earlier(hc), hc, later(hc)], 0).astype(BF16)
        return out_sum

    out_sum = jnp.zeros((C2, 128), F32)
    for step in range(16 // HEAD_GROUP):
        out_sum = head(step, out_sum)
    sums_ref[576:640, :] = out_sum
    hc_wide[0] = swapped(hc_wide[16])
    hc_wide[17] = swapped(hc_wide[1])

    for edge in (0, 17):
        mc_pad[edge] = jnp.zeros((C2, 128), BF16)

    def head_back(g):
        n = HEAD_GROUP
        window = hc_wide[pl.ds(n * g, n + 2)].reshape((n + 2) * 192, 128)
        grad = dot(w3b_ref[...], window).astype(BF16).astype(F32)
        mc = grad * slope_of(mid_pre[n * g : n * g + n].reshape(n * C2, 128))
        for k in range(n):
            one = mc[k * C2 : k * C2 + C2]
            mc_pad[n * g + k + 1] = one.astype(BF16)
            mc_pair[n * g + k] = jnp.concatenate([one, later(one)], 0).astype(BF16)

    for step in range(16 // HEAD_GROUP):
        head_back(step)
    mc_pair[16] = swapped(mc_pair[0])

    for edge in (0, 33):
        sc_pad[edge] = jnp.zeros((C1, 256), BF16)

    def mid_back(at):
        parts = []
        for r in range(at, at + BACK_BATCH):
            window = mc_pair[r : r + 2].reshape(256, 128)
            grad = dot(w2b_ref[...], window).astype(BF16)
            parts.append(jnp.concatenate([grad[0:64], grad[64:128]], 1))
        grads = dot(jnp.concatenate(parts, 0), inter_ref[...])
        for m in range(at // 2, (at + BACK_BATCH) // 2):
            grad = grads[128 * m - 64 * at : 128 * m - 64 * at + 128]
            cot = (grad * slope_of(stem_pre[4 * m : 4 * m + 4].reshape(128, 256))).astype(BF16)
            sc_pad[4 * m + 1 : 4 * m + 5] = cot.reshape(4, C1, 256)
            wire_ref[m, SHARE:WIRE_ROWS] = cot[:, 0:128]
            wire_ref[m + 8, SHARE:WIRE_ROWS] = cot[:, 128:256]

    for at in range(0, 16, BACK_BATCH):
        mid_back(at)

    total = None
    for k in range(0, 18, 2):
        left = jnp.concatenate([hc_pad[j : j + 3].reshape(192, 128) for j in (k, k + 1)], 1)
        right = jnp.concatenate([turned(hx[j]) for j in (k, k + 1)], 0)
        term = dot(left, right)
        total = term if total is None else total + term
    sums_ref[0:192, :] = total[:, 0:128]
    sums_ref[192:384, 0:64] = total[:, 128:192]
    total = None
    for k in range(17):
        term = dot_t(mx[2 * k : 2 * k + 2].reshape(192, 128), mc_pad[k : k + 2].reshape(128, 128))
        total = term if total is None else total + term
    sums_ref[384:576, :] = total
    total = None
    for k in range(33):
        term = dot(fx[2 * k : 2 * k + 2].reshape(192, 256), turned(sc_pad[k : k + 2].reshape(64, 256)))
        total = term if total is None else total + term
    sums_ref[192:384, 64:128] = total
    for s in range(SLABS):
        wire_ref[s, 0:SHARE] = sums_ref[s * SHARE : s * SHARE + SHARE, :].astype(BF16)


def scenario_pass(x, weights, out_weight, cotangent):
    out_shape = (
        jax.ShapeDtypeStruct((16, 128), F32),
        jax.ShapeDtypeStruct((SLABS, WIRE_ROWS, 128), BF16),
    )
    scratch = [
        pltpu.VMEM((SLABS * SHARE, 128), F32),
        pltpu.VMEM((66, 96, 256), BF16),
        pltpu.VMEM((32, C1, 256), F32),
        pltpu.VMEM((34, 96, 128), BF16),
        pltpu.VMEM((16, C2, 128), F32),
        pltpu.VMEM((18, 192, 128), BF16),
        pltpu.VMEM((18, 192, 128), BF16),
        pltpu.VMEM((20, C2, 128), BF16),
        pltpu.VMEM((17, 128, 128), BF16),
        pltpu.VMEM((18, C2, 128), BF16),
        pltpu.VMEM((34, C1, 256), BF16),
    ]
    whole = pl.BlockSpec(memory_space=pltpu.VMEM)
    return pl.pallas_call(
        scenario_kernel,
        out_shape=out_shape,
        in_specs=[whole] * 12,
        out_specs=(whole,) * 2,
        scratch_shapes=scratch,
        compiler_params=pltpu.CompilerParams(vmem_limit_bytes=32 << 20),
        cost_estimate=pl.CostEstimate(flops=4 * 10**9, bytes_accessed=4 << 20, transcendentals=10**6),
        name="scenario",
    )(x, *weights, *selections(), out_weight.reshape(C2, 1), cotangent)


def exchanged(value, axis):
    return lax.all_to_all(value, axis, split_axis=0, concat_axis=0, tiled=True)


def share_kernel(got_ref, out_ref):
    total = jnp.zeros((SHARE, 128), F32)
    for k in range(SLABS):
        total = total + got_ref[k, 0:SHARE].astype(F32)
    share = total.astype(BF16)
    for k in range(SLABS):
        out_ref[k] = share


def unpack_kernel(factor, sums_ref, stem_ref, mid_ref, head_ref, out_ref, wide):
    wide[...] = sums_ref[...].astype(F32) * factor
    for a in range(3):
        at = (2 - a) * C2
        head_ref[a, 0] = wide[at : at + C2, 0:64]
        head_ref[a, 1] = wide[at : at + C2, 64:128]
        head_ref[a, 2] = wide[192 + at : 192 + at + C2, 0:64]
        lanes = slice(0, 64) if a == 2 else slice(64, 128)
        for b in range(3):
            at = 384 + a % 2 * 96 + b * C1
            mid_ref[a, b] = wide[at : at + C1, lanes]
    for a in range(4):
        lanes = slice(64, 96) if a >= 2 else slice(96, 128)
        for c in range(CIN):
            rows = wide[pl.ds(192 + a % 2 * 96 + c, 4, stride=CIN), :]
            stem_ref[c, a] = rows[:, lanes]
    ones = jnp.full((8, 128), 1.0, BF16)
    out_ref[...] = dot_t(ones, sums_ref[576:640])[0:1] * factor


def on_chip(kernel, outs, scratch=(), name=None):
    whole = pl.BlockSpec(memory_space=pltpu.VMEM)
    single = not isinstance(outs, tuple)
    return lambda *args: pl.pallas_call(
        kernel,
        out_shape=outs,
        in_specs=[whole] * len(args),
        out_specs=whole if single else (whole,) * len(outs),
        scratch_shapes=scratch,
        compiler_params=pltpu.CompilerParams(vmem_limit_bytes=8 << 20),
        name=name,
    )(*args)


def summed_everywhere(got, factor):
    shares = jax.ShapeDtypeStruct((SLABS, SHARE, 128), BF16)
    share = on_chip(share_kernel, shares, name="lon_share")(got)
    share = on_chip(share_kernel, shares, name="rep_share")(exchanged(share, "rep"))
    sums = exchanged(share, "lon").reshape(SLABS * SHARE, 128)
    outs = (
        jax.ShapeDtypeStruct((CIN, 4, 4, C1), F32),
        jax.ShapeDtypeStruct((3, 3, C1, C2), F32),
        jax.ShapeDtypeStruct((3, 3, C2, C2), F32),
        jax.ShapeDtypeStruct((1, C2), F32),
    )
    scratch = [pltpu.VMEM((SLABS * SHARE, 128), F32)]
    stem, mid, head, out = on_chip(functools.partial(unpack_kernel, factor), outs, scratch, "unpack")(sums)
    return stem.transpose(3, 0, 1, 2), mid.transpose(3, 2, 0, 1), head.transpose(2, 3, 0, 1), out.reshape(C2)


def local(fields, stem_weight, mid_weight, head_weight, out_weight, pred_cotangent):
    x = exchanged(fields.reshape(SLABS, CIN * SLAB_LON, LAT), "lon")
    weights = kernel_weights(stem_weight, mid_weight, head_weight)
    cotangent = pred_cotangent.reshape(2, 16, 64).transpose(1, 0, 2).reshape(16, 128)
    prediction, wire = scenario_pass(x, weights, out_weight, cotangent)
    prediction = prediction.reshape(16, 2, 64).transpose(1, 0, 2).reshape(1, 32, 64)
    got = exchanged(wire, "lon")
    stem_cotangent = got[:, SHARE:].reshape(SLABS, 4, C1, 128).transpose(0, 2, 1, 3)
    factor = 1.0 / (fields.shape[0] * lax.axis_size("rep"))
    return (prediction, stem_cotangent, *summed_everywhere(got, factor))


def solution(mesh):
    placed = (P("rep", None, "lon", None), P(), P(), P(), P(), P(("rep", "lon"), None, None))
    return jax.shard_map(
        local,
        mesh=mesh,
        in_specs=placed,
        out_specs=(P(("rep", "lon"), None, None), P("rep", None, "lon", None), P(), P(), P(), P()),
        check_vma=False,
    )
```

```python
import functools

import jax
import jax.numpy as jnp
from jax import lax
from jax.experimental import pallas as pl
from jax.experimental.pallas import tpu as pltpu
from jax.sharding import PartitionSpec as P

BF16, F32 = jnp.bfloat16, jnp.float32
SLABS, CIN, SLAB_LON, LAT = 16, 24, 8, 256
C1, C2 = 32, 64
COT_ROWS, SHARE = 128, 40
WIRE_ROWS = SHARE + COT_ROWS
STEM_GROUP, STEM_BATCH, MID_GROUP, HEAD_GROUP = 4, 4, 2, 2
SLAB_BATCH, BACK_BATCH = 2, 8


def one_hot(shape, test):
    rows = lax.broadcasted_iota(jnp.int32, shape, 0)
    cols = lax.broadcasted_iota(jnp.int32, shape, 1)
    return jnp.where(test(rows, cols), 1.0, 0.0).astype(BF16)


def selections():
    regroup = one_hot(
        (CIN * SLAB_LON, CIN * SLAB_LON),
        lambda r, c: (r % CIN == c // SLAB_LON) & (r // CIN == c % SLAB_LON),
    )
    field_taps = one_hot((LAT, 256), lambda r, c: r == 2 * (c % 128) + c // 128)
    stem_taps = one_hot(
        (256, 256),
        lambda r, c: (r // 128 == c % 128 // 64) & (r % 128 == 2 * (c % 64) + c // 128),
    )
    interleave = one_hot(
        (256, 256),
        lambda r, c: (r % 128 // 64 == c // 128) & (c % 128 == 2 * (r % 64) + r // 128),
    )
    return regroup, field_taps, stem_taps, interleave


def toeplitz(rows, group, step):
    out, window, depth = rows.shape
    width = step * (group - 1) + window
    copies = [
        jnp.pad(rows, ((0, 0), (step * at, width - window - step * at), (0, 0))) for at in range(group)
    ]
    return jnp.stack(copies).reshape(group * out, width * depth)


def kernel_weights(stem_weight, mid_weight, head_weight):
    stem = stem_weight.transpose(0, 2, 3, 1).reshape(C1, 4, 4 * CIN)
    mid = mid_weight.transpose(0, 2, 3, 1).reshape(C2, 3, 3 * C1)
    head = head_weight.transpose(0, 2, 3, 1).reshape(C2, 3, 3 * C2)
    head_back = head_weight[:, :, ::-1, ::-1].transpose(1, 2, 3, 0).reshape(C2, 3, 3 * C2)
    none = jnp.zeros((C1, C2), mid_weight.dtype)
    blocks = []
    for lat_odd in (0, 1):
        for lon_odd in (0, 1):
            row = []
            for next_lon in (0, 1):
                for next_lat in (0, 1):
                    if next_lon > lon_odd or next_lat > lat_odd:
                        row.append(none)
                    else:
                        a = 1 if not lon_odd else 2 - 2 * next_lon
                        b = 1 if not lat_odd else 2 - 2 * next_lat
                        row.append(mid_weight[:, :, a, b].T)
            blocks.append(jnp.concatenate(row, 1))
    mid_back = jnp.concatenate(blocks, 0)
    return (
        toeplitz(stem, STEM_GROUP, 2),
        toeplitz(mid, MID_GROUP, 2),
        toeplitz(head, HEAD_GROUP, 1),
        toeplitz(head_back, HEAD_GROUP, 1),
        mid_back,
    )


def dot(left, right):
    return jnp.dot(left, right, preferred_element_type=F32)


def dot_t(left, right):
    return lax.dot_general(left, right, (((1,), (1,)), ((), ())), preferred_element_type=F32)


def turned(block):
    return block.astype(F32).T.astype(BF16)


def swapped(block):
    return pltpu.roll(block.astype(F32), 64, 1).astype(BF16)


def sigmoid(values):
    return 1.0 / (1.0 + jnp.exp(-values))


def slope_of(values):
    sigma = sigmoid(values)
    return sigma * (1.0 + values * (1.0 - sigma))


def scenario_kernel(
    x_ref, w1_ref, w2_ref, w3_ref, w3b_ref, w2b_ref, regroup_ref, ftaps_ref, staps_ref, inter_ref,
    ow_ref, pc_ref,
    pred_ref, wire_ref,
    sums_ref, fx, stem_pre, mx, mid_pre, hx, hc_wide, hc_pad, mc_pair, mc_pad, sc_pad,
):
    lane = lax.broadcasted_iota(jnp.int32, (C2, 128), 1) % 64
    first, last = lane == 0, lane == 63

    def earlier(block):
        return jnp.where(first, 0.0, pltpu.roll(block, 1, 1))

    def later(block):
        return jnp.where(last, 0.0, pltpu.roll(block, 127, 1))

    lat = lax.broadcasted_iota(jnp.int32, (192, 128), 1)

    def load_slabs(at):
        places = [(s, half) for s in range(at, at + SLAB_BATCH) for half in (0, 1)]
        parts = [dot(regroup_ref[...], x_ref[s + 8 * half]).astype(BF16) for s, half in places]
        all_taps = dot(jnp.concatenate(parts, 0), ftaps_ref[...])
        for k, (s, half) in enumerate(places):
            taps = all_taps[192 * k : 192 * k + 192]
            even, odd = taps[:, 0:128], taps[:, 128:256]
            before = jnp.where(lat == 0, 0.0, pltpu.roll(odd, 1, 1))
            after = jnp.where(lat == 127, 0.0, pltpu.roll(even, 127, 1))
            wide = jnp.concatenate([t.reshape(SLAB_LON, CIN, 128) for t in (before, even, odd, after)], 1)
            rows = slice(1 + s * SLAB_LON, 1 + s * SLAB_LON + SLAB_LON)
            fx[rows, :, half * 128 : half * 128 + 128] = wide.astype(BF16)

    for at in range(0, 8, SLAB_BATCH):
        load_slabs(at)
    fx[0, :, 0:128] = fx[64, :, 128:256]
    fx[0, :, 128:256] = fx[64, :, 0:128]
    fx[65, :, 0:128] = fx[1, :, 128:256]
    fx[65, :, 128:256] = fx[1, :, 0:128]

    def stem(g):
        n = STEM_GROUP
        window = fx[pl.ds(2 * n * g, 2 * n + 2)].reshape((2 * n + 2) * 96, 256)
        pre = dot(w1_ref[...], window)
        stem_pre[n * g : n * g + n] = pre.reshape(n, C1, 256)
        return (pre * sigmoid(pre)).astype(BF16)

    def stem_taps(acts, at):
        n = STEM_GROUP * len(acts)
        taps = dot(jnp.concatenate(acts, 0), staps_ref[...])
        even, odd = taps[:, 0:128], taps[:, 128:256]
        lat = lax.broadcasted_iota(jnp.int32, odd.shape, 1) % 64
        before = jnp.where(lat == 0, 0.0, pltpu.roll(odd, 1, 1))
        wide = jnp.concatenate([t.reshape(n, C1, 128) for t in (before, even, odd)], 1)
        mx[1 + at : 1 + at + n] = wide.astype(BF16)

    for at in range(0, 32 // STEM_GROUP, STEM_BATCH):
        stem_taps([stem(at + k) for k in range(STEM_BATCH)], at * STEM_GROUP)
    mx[0] = swapped(mx[32])
    mx[33] = jnp.zeros((96, 128), BF16)

    def mid(g):
        n = MID_GROUP
        window = mx[pl.ds(2 * n * g, 2 * n + 1)].reshape((2 * n + 1) * 96, 128)
        pre = dot(w2_ref[...], window)
        mid_pre[n * g : n * g + n] = pre.reshape(n, C2, 128)
        act = pre * sigmoid(pre)
        for k in range(n):
            one = act[k * C2 : k * C2 + C2]
            hx[n * g + k + 1] = jnp.concatenate([earlier(one), one, later(one)], 0).astype(BF16)

    for step in range(16 // MID_GROUP):
        mid(step)
    hx[0] = swapped(hx[16])
    hx[17] = swapped(hx[1])

    for edge in (0, 1, 18, 19):
        hc_pad[edge] = jnp.zeros((C2, 128), BF16)
    out_w = jnp.broadcast_to(ow_ref[...], (C2, 128))

    def head(g, out_sum):
        n = HEAD_GROUP
        window = hx[pl.ds(n * g, n + 2)].reshape((n + 2) * 192, 128)
        pre = dot(w3_ref[...], window)
        sigma = sigmoid(pre)
        act = (pre * sigma).astype(BF16).astype(F32)
        bend = sigma * (1.0 + pre * (1.0 - sigma))
        for k in range(n):
            r = n * g + k
            here = slice(k * C2, k * C2 + C2)
            cot = jnp.broadcast_to(pc_ref[r : r + 1, :], (C2, 128))
            pred_ref[r : r + 1, :] = jnp.sum(out_w * act[here], 0, keepdims=True)
            out_sum = out_sum + cot * act[here]
            hc = (cot * out_w) * bend[here]
            hc_pad[r + 2] = hc.astype(BF16)
            hc_wide[r + 1] = jnp.concatenate([earlier(hc), hc, later(hc)], 0).astype(BF16)
        return out_sum

    out_sum = jnp.zeros((C2, 128), F32)
    for step in range(16 // HEAD_GROUP):
        out_sum = head(step, out_sum)
    sums_ref[576:640, :] = out_sum
    hc_wide[0] = swapped(hc_wide[16])
    hc_wide[17] = swapped(hc_wide[1])

    for edge in (0, 17):
        mc_pad[edge] = jnp.zeros((C2, 128), BF16)

    def head_back(g):
        n = HEAD_GROUP
        window = hc_wide[pl.ds(n * g, n + 2)].reshape((n + 2) * 192, 128)
        grad = dot(w3b_ref[...], window).astype(BF16).astype(F32)
        mc = grad * slope_of(mid_pre[n * g : n * g + n].reshape(n * C2, 128))
        for k in range(n):
            one = mc[k * C2 : k * C2 + C2]
            mc_pad[n * g + k + 1] = one.astype(BF16)
            mc_pair[n * g + k] = jnp.concatenate([one, later(one)], 0).astype(BF16)

    for step in range(16 // HEAD_GROUP):
        head_back(step)
    mc_pair[16] = swapped(mc_pair[0])

    for edge in (0, 33):
        sc_pad[edge] = jnp.zeros((C1, 256), BF16)

    def mid_back(at):
        parts = []
        for r in range(at, at + BACK_BATCH):
            window = mc_pair[r : r + 2].reshape(256, 128)
            grad = dot(w2b_ref[...], window).astype(BF16)
            parts.append(jnp.concatenate([grad[0:64], grad[64:128]], 1))
        grads = dot(jnp.concatenate(parts, 0), inter_ref[...])
        for m in range(at // 2, (at + BACK_BATCH) // 2):
            grad = grads[128 * m - 64 * at : 128 * m - 64 * at + 128]
            cot = (grad * slope_of(stem_pre[4 * m : 4 * m + 4].reshape(128, 256))).astype(BF16)
            sc_pad[4 * m + 1 : 4 * m + 5] = cot.reshape(4, C1, 256)
            wire_ref[m, SHARE:WIRE_ROWS] = cot[:, 0:128]
            wire_ref[m + 8, SHARE:WIRE_ROWS] = cot[:, 128:256]

    for at in range(0, 16, BACK_BATCH):
        mid_back(at)

    total = None
    for k in range(0, 18, 2):
        left = jnp.concatenate([hc_pad[j : j + 3].reshape(192, 128) for j in (k, k + 1)], 1)
        right = jnp.concatenate([turned(hx[j]) for j in (k, k + 1)], 0)
        term = dot(left, right)
        total = term if total is None else total + term
    sums_ref[0:192, :] = total[:, 0:128]
    sums_ref[192:384, 0:64] = total[:, 128:192]
    total = None
    for k in range(17):
        term = dot_t(mx[2 * k : 2 * k + 2].reshape(192, 128), mc_pad[k : k + 2].reshape(128, 128))
        total = term if total is None else total + term
    sums_ref[384:576, :] = total
    total = None
    for k in range(33):
        term = dot(fx[2 * k : 2 * k + 2].reshape(192, 256), turned(sc_pad[k : k + 2].reshape(64, 256)))
        total = term if total is None else total + term
    sums_ref[192:384, 64:128] = total
    for s in range(SLABS):
        wire_ref[s, 0:SHARE] = sums_ref[s * SHARE : s * SHARE + SHARE, :].astype(BF16)


def scenario_pass(x, weights, out_weight, cotangent):
    out_shape = (
        jax.ShapeDtypeStruct((16, 128), F32),
        jax.ShapeDtypeStruct((SLABS, WIRE_ROWS, 128), BF16),
    )
    scratch = [
        pltpu.VMEM((SLABS * SHARE, 128), F32),
        pltpu.VMEM((66, 96, 256), BF16),
        pltpu.VMEM((32, C1, 256), F32),
        pltpu.VMEM((34, 96, 128), BF16),
        pltpu.VMEM((16, C2, 128), F32),
        pltpu.VMEM((18, 192, 128), BF16),
        pltpu.VMEM((18, 192, 128), BF16),
        pltpu.VMEM((20, C2, 128), BF16),
        pltpu.VMEM((17, 128, 128), BF16),
        pltpu.VMEM((18, C2, 128), BF16),
        pltpu.VMEM((34, C1, 256), BF16),
    ]
    whole = pl.BlockSpec(memory_space=pltpu.VMEM)
    return pl.pallas_call(
        scenario_kernel,
        out_shape=out_shape,
        in_specs=[whole] * 12,
        out_specs=(whole,) * 2,
        scratch_shapes=scratch,
        compiler_params=pltpu.CompilerParams(vmem_limit_bytes=32 << 20),
        cost_estimate=pl.CostEstimate(flops=4 * 10**9, bytes_accessed=4 << 20, transcendentals=10**6),
        name="scenario",
    )(x, *weights, *selections(), out_weight.reshape(C2, 1), cotangent)


def exchanged(value, axis, groups=None):
    return lax.all_to_all(
        value, axis, split_axis=0, concat_axis=0, tiled=True, axis_index_groups=groups
    )


def share_kernel(got_ref, out_ref):
    total = jnp.zeros((SHARE, 128), F32)
    for k in range(got_ref.shape[0]):
        total = total + got_ref[k, 0:SHARE].astype(F32)
    share = total.astype(BF16)
    for k in range(out_ref.shape[0]):
        out_ref[k] = share


def unpack_kernel(factor, sums_ref, stem_ref, mid_ref, head_ref, out_ref, wide):
    rows = SLABS * SHARE
    wide[...] = (sums_ref[0:rows].astype(F32) + sums_ref[rows : 2 * rows].astype(F32)) * factor
    for a in range(3):
        at = (2 - a) * C2
        head_ref[a, 0] = wide[at : at + C2, 0:64]
        head_ref[a, 1] = wide[at : at + C2, 64:128]
        head_ref[a, 2] = wide[192 + at : 192 + at + C2, 0:64]
        lanes = slice(0, 64) if a == 2 else slice(64, 128)
        for b in range(3):
            at = 384 + a % 2 * 96 + b * C1
            mid_ref[a, b] = wide[at : at + C1, lanes]
    for a in range(4):
        lanes = slice(64, 96) if a >= 2 else slice(96, 128)
        for c in range(CIN):
            taps = wide[pl.ds(192 + a % 2 * 96 + c, 4, stride=CIN), :]
            stem_ref[c, a] = taps[:, lanes]
    ones = jnp.full((8, 128), 1.0, BF16)
    out_sums = [dot_t(ones, sums_ref[at + 576 : at + 640])[0:1] for at in (0, rows)]
    out_ref[...] = (out_sums[0] + out_sums[1]) * factor


def on_chip(kernel, outs, scratch=(), name=None):
    whole = pl.BlockSpec(memory_space=pltpu.VMEM)
    single = not isinstance(outs, tuple)
    return lambda *args: pl.pallas_call(
        kernel,
        out_shape=outs,
        in_specs=[whole] * len(args),
        out_specs=whole if single else (whole,) * len(outs),
        scratch_shapes=scratch,
        compiler_params=pltpu.CompilerParams(vmem_limit_bytes=8 << 20),
        name=name,
    )(*args)


def summed_everywhere(got, factor):
    lon, rep = lax.axis_size("lon"), lax.axis_size("rep")
    lines = [list(range(parity, rep, 2)) for parity in (0, 1)]
    planes = [
        [(2 * z + parity) * lon + k for parity in (0, 1) for k in range(lon)] for z in range(rep // 2)
    ]
    one_line = jax.ShapeDtypeStruct((rep // 2, SHARE, 128), BF16)
    one_plane = jax.ShapeDtypeStruct((2 * lon, SHARE, 128), BF16)
    share = on_chip(share_kernel, one_line, name="lon_share")(got)
    share = on_chip(share_kernel, one_plane, name="line_share")(exchanged(share, "rep", lines))
    sums = exchanged(share, ("rep", "lon"), planes).reshape(2 * SLABS * SHARE, 128)
    outs = (
        jax.ShapeDtypeStruct((CIN, 4, 4, C1), F32),
        jax.ShapeDtypeStruct((3, 3, C1, C2), F32),
        jax.ShapeDtypeStruct((3, 3, C2, C2), F32),
        jax.ShapeDtypeStruct((1, C2), F32),
    )
    scratch = [pltpu.VMEM((SLABS * SHARE, 128), F32)]
    stem, mid, head, out = on_chip(functools.partial(unpack_kernel, factor), outs, scratch, "unpack")(sums)
    return stem.transpose(3, 0, 1, 2), mid.transpose(3, 2, 0, 1), head.transpose(2, 3, 0, 1), out.reshape(C2)


def local(fields, stem_weight, mid_weight, head_weight, out_weight, pred_cotangent):
    x = exchanged(fields.reshape(SLABS, CIN * SLAB_LON, LAT), "lon")
    weights = kernel_weights(stem_weight, mid_weight, head_weight)
    cotangent = pred_cotangent.reshape(2, 16, 64).transpose(1, 0, 2).reshape(16, 128)
    prediction, wire = scenario_pass(x, weights, out_weight, cotangent)
    prediction = prediction.reshape(16, 2, 64).transpose(1, 0, 2).reshape(1, 32, 64)
    got = exchanged(wire, "lon")
    stem_cotangent = got[:, SHARE:].reshape(SLABS, 4, C1, 128).transpose(0, 2, 1, 3)
    factor = 1.0 / (fields.shape[0] * lax.axis_size("rep"))
    return (prediction, stem_cotangent, *summed_everywhere(got, factor))


def solution(mesh):
    placed = (P("rep", None, "lon", None), P(), P(), P(), P(), P(("rep", "lon"), None, None))
    return jax.shard_map(
        local,
        mesh=mesh,
        in_specs=placed,
        out_specs=(P(("rep", "lon"), None, None), P("rep", None, "lon", None), P(), P(), P(), P()),
        check_vma=False,
    )
```

```python
import functools

import jax
import jax.numpy as jnp
from jax import lax
from jax.experimental import pallas as pl
from jax.experimental.pallas import tpu as pltpu
from jax.sharding import PartitionSpec as P

BF16, F32 = jnp.bfloat16, jnp.float32
SLABS, CIN, SLAB_LON, LAT = 16, 24, 8, 256
C1, C2 = 32, 64
COT_ROWS, SHARE = 128, 40
WIRE_ROWS = SHARE + COT_ROWS
STEM_GROUP, STEM_BATCH, MID_GROUP, HEAD_GROUP = 4, 4, 2, 2
SLAB_BATCH, BACK_BATCH = 2, 8


def one_hot(shape, test):
    rows = lax.broadcasted_iota(jnp.int32, shape, 0)
    cols = lax.broadcasted_iota(jnp.int32, shape, 1)
    return jnp.where(test(rows, cols), 1.0, 0.0).astype(BF16)


def selections():
    regroup = one_hot(
        (CIN * SLAB_LON, CIN * SLAB_LON),
        lambda r, c: (r % CIN == c // SLAB_LON) & (r // CIN == c % SLAB_LON),
    )
    field_taps = one_hot((LAT, 256), lambda r, c: r == 2 * (c % 128) + c // 128)
    stem_taps = one_hot(
        (256, 256),
        lambda r, c: (r // 128 == c % 128 // 64) & (r % 128 == 2 * (c % 64) + c // 128),
    )
    interleave = one_hot(
        (256, 256),
        lambda r, c: (r % 128 // 64 == c // 128) & (c % 128 == 2 * (r % 64) + r // 128),
    )
    return regroup, field_taps, stem_taps, interleave


def toeplitz(rows, group, step):
    out, window, depth = rows.shape
    width = step * (group - 1) + window
    copies = [
        jnp.pad(rows, ((0, 0), (step * at, width - window - step * at), (0, 0))) for at in range(group)
    ]
    return jnp.stack(copies).reshape(group * out, width * depth)


def kernel_weights(stem_weight, mid_weight, head_weight):
    stem = stem_weight.transpose(0, 2, 3, 1).reshape(C1, 4, 4 * CIN)
    mid = mid_weight.transpose(0, 2, 3, 1).reshape(C2, 3, 3 * C1)
    head = head_weight.transpose(0, 2, 3, 1).reshape(C2, 3, 3 * C2)
    head_back = head_weight[:, :, ::-1, ::-1].transpose(1, 2, 3, 0).reshape(C2, 3, 3 * C2)
    none = jnp.zeros((C1, C2), mid_weight.dtype)
    blocks = []
    for lat_odd in (0, 1):
        for lon_odd in (0, 1):
            row = []
            for next_lon in (0, 1):
                for next_lat in (0, 1):
                    if next_lon > lon_odd or next_lat > lat_odd:
                        row.append(none)
                    else:
                        a = 1 if not lon_odd else 2 - 2 * next_lon
                        b = 1 if not lat_odd else 2 - 2 * next_lat
                        row.append(mid_weight[:, :, a, b].T)
            blocks.append(jnp.concatenate(row, 1))
    mid_back = jnp.concatenate(blocks, 0)
    return (
        toeplitz(stem, STEM_GROUP, 2),
        toeplitz(mid, MID_GROUP, 2),
        toeplitz(head, HEAD_GROUP, 1),
        toeplitz(head_back, HEAD_GROUP, 1),
        mid_back,
    )


def dot(left, right):
    return jnp.dot(left, right, preferred_element_type=F32)


def dot_t(left, right):
    return lax.dot_general(left, right, (((1,), (1,)), ((), ())), preferred_element_type=F32)


def side_by_side(weights, windows):
    out = []
    for at in range(0, len(windows), 2):
        both = dot(weights, jnp.concatenate(windows[at : at + 2], 1))
        out += [both[:, 0:128], both[:, 128:256]]
    return out


def turned(block):
    return block.astype(F32).T.astype(BF16)


def swapped(block):
    return pltpu.roll(block.astype(F32), 64, 1).astype(BF16)


def sigmoid(values):
    return 1.0 / (1.0 + jnp.exp(-values))


def slope_of(values):
    sigma = sigmoid(values)
    return sigma * (1.0 + values * (1.0 - sigma))


def scenario_kernel(
    x_ref, w1_ref, w2_ref, w3_ref, w3b_ref, w2b_ref, regroup_ref, ftaps_ref, staps_ref, inter_ref,
    ow_ref, pc_ref,
    pred_ref, wire_ref,
    sums_ref, fx, stem_pre, mx, mid_pre, hx, hc_wide, hc_pad, mc_pair, mc_pad, sc_pad,
):
    lane = lax.broadcasted_iota(jnp.int32, (C2, 128), 1) % 64
    first, last = lane == 0, lane == 63

    def earlier(block):
        return jnp.where(first, 0.0, pltpu.roll(block, 1, 1))

    def later(block):
        return jnp.where(last, 0.0, pltpu.roll(block, 127, 1))

    lat = lax.broadcasted_iota(jnp.int32, (192, 128), 1)

    def load_slabs(at):
        places = [(s, half) for s in range(at, at + SLAB_BATCH) for half in (0, 1)]
        parts = [dot(regroup_ref[...], x_ref[s + 8 * half]).astype(BF16) for s, half in places]
        all_taps = dot(jnp.concatenate(parts, 0), ftaps_ref[...])
        for k, (s, half) in enumerate(places):
            taps = all_taps[192 * k : 192 * k + 192]
            even, odd = taps[:, 0:128], taps[:, 128:256]
            before = jnp.where(lat == 0, 0.0, pltpu.roll(odd, 1, 1))
            after = jnp.where(lat == 127, 0.0, pltpu.roll(even, 127, 1))
            wide = jnp.concatenate([t.reshape(SLAB_LON, CIN, 128) for t in (before, even, odd, after)], 1)
            rows = slice(1 + s * SLAB_LON, 1 + s * SLAB_LON + SLAB_LON)
            fx[rows, :, half * 128 : half * 128 + 128] = wide.astype(BF16)

    for at in range(0, 8, SLAB_BATCH):
        load_slabs(at)
    fx[0, :, 0:128] = fx[64, :, 128:256]
    fx[0, :, 128:256] = fx[64, :, 0:128]
    fx[65, :, 0:128] = fx[1, :, 128:256]
    fx[65, :, 128:256] = fx[1, :, 0:128]

    def stem(g):
        n = STEM_GROUP
        window = fx[pl.ds(2 * n * g, 2 * n + 2)].reshape((2 * n + 2) * 96, 256)
        pre = dot(w1_ref[...], window)
        stem_pre[n * g : n * g + n] = pre.reshape(n, C1, 256)
        return (pre * sigmoid(pre)).astype(BF16)

    def stem_taps(acts, at):
        n = STEM_GROUP * len(acts)
        taps = dot(jnp.concatenate(acts, 0), staps_ref[...])
        even, odd = taps[:, 0:128], taps[:, 128:256]
        lat = lax.broadcasted_iota(jnp.int32, odd.shape, 1) % 64
        before = jnp.where(lat == 0, 0.0, pltpu.roll(odd, 1, 1))
        wide = jnp.concatenate([t.reshape(n, C1, 128) for t in (before, even, odd)], 1)
        mx[1 + at : 1 + at + n] = wide.astype(BF16)

    for at in range(0, 32 // STEM_GROUP, STEM_BATCH):
        stem_taps([stem(at + k) for k in range(STEM_BATCH)], at * STEM_GROUP)
    mx[0] = swapped(mx[32])
    mx[33] = jnp.zeros((96, 128), BF16)

    def mid_window(g):
        n = MID_GROUP
        return mx[2 * n * g : 2 * n * g + 2 * n + 1].reshape((2 * n + 1) * 96, 128)

    def mid(g, pre):
        n = MID_GROUP
        mid_pre[n * g : n * g + n] = pre.reshape(n, C2, 128)
        act = pre * sigmoid(pre)
        for k in range(n):
            one = act[k * C2 : k * C2 + C2]
            hx[n * g + k + 1] = jnp.concatenate([earlier(one), one, later(one)], 0).astype(BF16)

    for step in range(0, 16 // MID_GROUP, 2):
        pres = side_by_side(w2_ref[...], [mid_window(step), mid_window(step + 1)])
        mid(step, pres[0])
        mid(step + 1, pres[1])
    hx[0] = swapped(hx[16])
    hx[17] = swapped(hx[1])

    for edge in (0, 1, 18, 19):
        hc_pad[edge] = jnp.zeros((C2, 128), BF16)
    out_w = jnp.broadcast_to(ow_ref[...], (C2, 128))

    def head_window(maps, g):
        n = HEAD_GROUP
        return maps[n * g : n * g + n + 2].reshape((n + 2) * 192, 128)

    def head(g, pre, out_sum):
        n = HEAD_GROUP
        sigma = sigmoid(pre)
        act = (pre * sigma).astype(BF16).astype(F32)
        bend = sigma * (1.0 + pre * (1.0 - sigma))
        for k in range(n):
            r = n * g + k
            here = slice(k * C2, k * C2 + C2)
            cot = jnp.broadcast_to(pc_ref[r : r + 1, :], (C2, 128))
            pred_ref[r : r + 1, :] = jnp.sum(out_w * act[here], 0, keepdims=True)
            out_sum = out_sum + cot * act[here]
            hc = (cot * out_w) * bend[here]
            hc_pad[r + 2] = hc.astype(BF16)
            hc_wide[r + 1] = jnp.concatenate([earlier(hc), hc, later(hc)], 0).astype(BF16)
        return out_sum

    out_sum = jnp.zeros((C2, 128), F32)
    for step in range(0, 16 // HEAD_GROUP, 2):
        pres = side_by_side(w3_ref[...], [head_window(hx, step), head_window(hx, step + 1)])
        out_sum = head(step, pres[0], out_sum)
        out_sum = head(step + 1, pres[1], out_sum)
    sums_ref[576:640, :] = out_sum
    hc_wide[0] = swapped(hc_wide[16])
    hc_wide[17] = swapped(hc_wide[1])

    for edge in (0, 17):
        mc_pad[edge] = jnp.zeros((C2, 128), BF16)

    def head_back(g, grad):
        n = HEAD_GROUP
        grad = grad.astype(BF16).astype(F32)
        mc = grad * slope_of(mid_pre[n * g : n * g + n].reshape(n * C2, 128))
        for k in range(n):
            one = mc[k * C2 : k * C2 + C2]
            mc_pad[n * g + k + 1] = one.astype(BF16)
            mc_pair[n * g + k] = jnp.concatenate([one, later(one)], 0).astype(BF16)

    for step in range(0, 16 // HEAD_GROUP, 2):
        grads = side_by_side(w3b_ref[...], [head_window(hc_wide, step), head_window(hc_wide, step + 1)])
        head_back(step, grads[0])
        head_back(step + 1, grads[1])
    mc_pair[16] = swapped(mc_pair[0])

    for edge in (0, 33):
        sc_pad[edge] = jnp.zeros((C1, 256), BF16)

    def mid_back(at):
        parts = []
        windows = [mc_pair[r : r + 2].reshape(256, 128) for r in range(at, at + BACK_BATCH)]
        for grad in side_by_side(w2b_ref[...], windows):
            grad = grad.astype(BF16)
            parts.append(jnp.concatenate([grad[0:64], grad[64:128]], 1))
        grads = dot(jnp.concatenate(parts, 0), inter_ref[...])
        for m in range(at // 2, (at + BACK_BATCH) // 2):
            grad = grads[128 * m - 64 * at : 128 * m - 64 * at + 128]
            cot = (grad * slope_of(stem_pre[4 * m : 4 * m + 4].reshape(128, 256))).astype(BF16)
            sc_pad[4 * m + 1 : 4 * m + 5] = cot.reshape(4, C1, 256)
            wire_ref[m, SHARE:WIRE_ROWS] = cot[:, 0:128]
            wire_ref[m + 8, SHARE:WIRE_ROWS] = cot[:, 128:256]

    for at in range(0, 16, BACK_BATCH):
        mid_back(at)

    total = None
    for k in range(0, 18, 2):
        left = jnp.concatenate([hc_pad[j : j + 3].reshape(192, 128) for j in (k, k + 1)], 1)
        right = jnp.concatenate([turned(hx[j]) for j in (k, k + 1)], 0)
        term = dot(left, right)
        total = term if total is None else total + term
    sums_ref[0:192, :] = total[:, 0:128]
    sums_ref[192:384, 0:64] = total[:, 128:192]
    total = None
    for k in range(17):
        term = dot_t(mx[2 * k : 2 * k + 2].reshape(192, 128), mc_pad[k : k + 2].reshape(128, 128))
        total = term if total is None else total + term
    sums_ref[384:576, :] = total
    total = None
    for k in range(33):
        term = dot(fx[2 * k : 2 * k + 2].reshape(192, 256), turned(sc_pad[k : k + 2].reshape(64, 256)))
        total = term if total is None else total + term
    sums_ref[192:384, 64:128] = total
    for s in range(SLABS):
        wire_ref[s, 0:SHARE] = sums_ref[s * SHARE : s * SHARE + SHARE, :].astype(BF16)


def scenario_pass(x, weights, out_weight, cotangent):
    out_shape = (
        jax.ShapeDtypeStruct((16, 128), F32),
        jax.ShapeDtypeStruct((SLABS, WIRE_ROWS, 128), BF16),
    )
    scratch = [
        pltpu.VMEM((SLABS * SHARE, 128), F32),
        pltpu.VMEM((66, 96, 256), BF16),
        pltpu.VMEM((32, C1, 256), F32),
        pltpu.VMEM((34, 96, 128), BF16),
        pltpu.VMEM((16, C2, 128), F32),
        pltpu.VMEM((18, 192, 128), BF16),
        pltpu.VMEM((18, 192, 128), BF16),
        pltpu.VMEM((20, C2, 128), BF16),
        pltpu.VMEM((17, 128, 128), BF16),
        pltpu.VMEM((18, C2, 128), BF16),
        pltpu.VMEM((34, C1, 256), BF16),
    ]
    whole = pl.BlockSpec(memory_space=pltpu.VMEM)
    return pl.pallas_call(
        scenario_kernel,
        out_shape=out_shape,
        in_specs=[whole] * 12,
        out_specs=(whole,) * 2,
        scratch_shapes=scratch,
        compiler_params=pltpu.CompilerParams(vmem_limit_bytes=32 << 20),
        cost_estimate=pl.CostEstimate(flops=4 * 10**9, bytes_accessed=4 << 20, transcendentals=10**6),
        name="scenario",
    )(x, *weights, *selections(), out_weight.reshape(C2, 1), cotangent)


def exchanged(value, axis, groups=None):
    return lax.all_to_all(
        value, axis, split_axis=0, concat_axis=0, tiled=True, axis_index_groups=groups
    )


def share_kernel(got_ref, out_ref):
    total = jnp.zeros((SHARE, 128), F32)
    for k in range(got_ref.shape[0]):
        total = total + got_ref[k, 0:SHARE].astype(F32)
    share = total.astype(BF16)
    for k in range(out_ref.shape[0]):
        out_ref[k] = share


def unpack_kernel(factor, sums_ref, stem_ref, mid_ref, head_ref, out_ref, wide):
    rows = SLABS * SHARE
    wide[...] = (sums_ref[0:rows].astype(F32) + sums_ref[rows : 2 * rows].astype(F32)) * factor
    for a in range(3):
        at = (2 - a) * C2
        head_ref[a, 0] = wide[at : at + C2, 0:64]
        head_ref[a, 1] = wide[at : at + C2, 64:128]
        head_ref[a, 2] = wide[192 + at : 192 + at + C2, 0:64]
        lanes = slice(0, 64) if a == 2 else slice(64, 128)
        for b in range(3):
            at = 384 + a % 2 * 96 + b * C1
            mid_ref[a, b] = wide[at : at + C1, lanes]
    for a in range(4):
        lanes = slice(64, 96) if a >= 2 else slice(96, 128)
        for c in range(CIN):
            taps = wide[pl.ds(192 + a % 2 * 96 + c, 4, stride=CIN), :]
            stem_ref[c, a] = taps[:, lanes]
    ones = jnp.full((8, 128), 1.0, BF16)
    out_sums = [dot_t(ones, sums_ref[at + 576 : at + 640])[0:1] for at in (0, rows)]
    out_ref[...] = (out_sums[0] + out_sums[1]) * factor


def on_chip(kernel, outs, scratch=(), name=None):
    whole = pl.BlockSpec(memory_space=pltpu.VMEM)
    single = not isinstance(outs, tuple)
    return lambda *args: pl.pallas_call(
        kernel,
        out_shape=outs,
        in_specs=[whole] * len(args),
        out_specs=whole if single else (whole,) * len(outs),
        scratch_shapes=scratch,
        compiler_params=pltpu.CompilerParams(vmem_limit_bytes=8 << 20),
        name=name,
    )(*args)


def summed_everywhere(got, factor):
    lon, rep = lax.axis_size("lon"), lax.axis_size("rep")
    lines = [list(range(parity, rep, 2)) for parity in (0, 1)]
    planes = [
        [(2 * z + parity) * lon + k for parity in (0, 1) for k in range(lon)] for z in range(rep // 2)
    ]
    one_line = jax.ShapeDtypeStruct((rep // 2, SHARE, 128), BF16)
    one_plane = jax.ShapeDtypeStruct((2 * lon, SHARE, 128), BF16)
    share = on_chip(share_kernel, one_line, name="lon_share")(got)
    share = on_chip(share_kernel, one_plane, name="line_share")(exchanged(share, "rep", lines))
    sums = exchanged(share, ("rep", "lon"), planes).reshape(2 * SLABS * SHARE, 128)
    outs = (
        jax.ShapeDtypeStruct((CIN, 4, 4, C1), F32),
        jax.ShapeDtypeStruct((3, 3, C1, C2), F32),
        jax.ShapeDtypeStruct((3, 3, C2, C2), F32),
        jax.ShapeDtypeStruct((1, C2), F32),
    )
    scratch = [pltpu.VMEM((SLABS * SHARE, 128), F32)]
    stem, mid, head, out = on_chip(functools.partial(unpack_kernel, factor), outs, scratch, "unpack")(sums)
    return stem.transpose(3, 0, 1, 2), mid.transpose(3, 2, 0, 1), head.transpose(2, 3, 0, 1), out.reshape(C2)


def local(fields, stem_weight, mid_weight, head_weight, out_weight, pred_cotangent):
    x = exchanged(fields.reshape(SLABS, CIN * SLAB_LON, LAT), "lon")
    weights = kernel_weights(stem_weight, mid_weight, head_weight)
    cotangent = pred_cotangent.reshape(2, 16, 64).transpose(1, 0, 2).reshape(16, 128)
    prediction, wire = scenario_pass(x, weights, out_weight, cotangent)
    prediction = prediction.reshape(16, 2, 64).transpose(1, 0, 2).reshape(1, 32, 64)
    got = exchanged(wire, "lon")
    stem_cotangent = got[:, SHARE:].reshape(SLABS, 4, C1, 128).transpose(0, 2, 1, 3)
    factor = 1.0 / (fields.shape[0] * lax.axis_size("rep"))
    return (prediction, stem_cotangent, *summed_everywhere(got, factor))


def solution(mesh):
    placed = (P("rep", None, "lon", None), P(), P(), P(), P(), P(("rep", "lon"), None, None))
    return jax.shard_map(
        local,
        mesh=mesh,
        in_specs=placed,
        out_specs=(P(("rep", "lon"), None, None), P("rep", None, "lon", None), P(), P(), P(), P()),
        check_vma=False,
    )
```

```python
import functools

import jax
import jax.numpy as jnp
from jax import lax
from jax.experimental import pallas as pl
from jax.experimental.pallas import tpu as pltpu
from jax.sharding import PartitionSpec as P

BF16, F32 = jnp.bfloat16, jnp.float32
SLABS, CIN, SLAB_LON, LAT = 16, 24, 8, 256
C1, C2 = 32, 64
COT_ROWS, SHARE = 128, 40
WIRE_ROWS = SHARE + COT_ROWS
STEM_GROUP, STEM_BATCH, MID_GROUP, HEAD_GROUP = 4, 4, 1, 1
SLAB_BATCH, BACK_BATCH = 2, 8


def one_hot(shape, test):
    rows = lax.broadcasted_iota(jnp.int32, shape, 0)
    cols = lax.broadcasted_iota(jnp.int32, shape, 1)
    return jnp.where(test(rows, cols), 1.0, 0.0).astype(BF16)


def selections():
    regroup = one_hot(
        (CIN * SLAB_LON, CIN * SLAB_LON),
        lambda r, c: (r % CIN == c // SLAB_LON) & (r // CIN == c % SLAB_LON),
    )
    field_taps = one_hot((LAT, 256), lambda r, c: r == 2 * (c % 128) + c // 128)
    stem_taps = one_hot(
        (256, 256),
        lambda r, c: (r // 128 == c % 128 // 64) & (r % 128 == 2 * (c % 64) + c // 128),
    )
    interleave = one_hot(
        (256, 256),
        lambda r, c: (r % 128 // 64 == c // 128) & (c % 128 == 2 * (r % 64) + r // 128),
    )
    return regroup, field_taps, stem_taps, interleave


def toeplitz(rows, group, step):
    out, window, depth = rows.shape
    width = step * (group - 1) + window
    copies = [
        jnp.pad(rows, ((0, 0), (step * at, width - window - step * at), (0, 0))) for at in range(group)
    ]
    return jnp.stack(copies).reshape(group * out, width * depth)


def kernel_weights(stem_weight, mid_weight, head_weight):
    stem = stem_weight.transpose(0, 2, 3, 1).reshape(C1, 4, 4 * CIN)
    mid = mid_weight.transpose(0, 2, 3, 1).reshape(C2, 3, 3 * C1)
    head = head_weight.transpose(0, 2, 3, 1).reshape(C2, 3, 3 * C2)
    head_back = head_weight[:, :, ::-1, ::-1].transpose(1, 2, 3, 0).reshape(C2, 3, 3 * C2)
    none = jnp.zeros((C1, C2), mid_weight.dtype)
    blocks = []
    for lat_odd in (0, 1):
        for lon_odd in (0, 1):
            row = []
            for next_lon in (0, 1):
                for next_lat in (0, 1):
                    if next_lon > lon_odd or next_lat > lat_odd:
                        row.append(none)
                    else:
                        a = 1 if not lon_odd else 2 - 2 * next_lon
                        b = 1 if not lat_odd else 2 - 2 * next_lat
                        row.append(mid_weight[:, :, a, b].T)
            blocks.append(jnp.concatenate(row, 1))
    mid_back = jnp.concatenate(blocks, 0)
    return (
        toeplitz(stem, STEM_GROUP, 2),
        toeplitz(mid, MID_GROUP, 2),
        toeplitz(head, HEAD_GROUP, 1),
        toeplitz(head_back, HEAD_GROUP, 1),
        mid_back,
    )


def dot(left, right):
    return jnp.dot(left, right, preferred_element_type=F32)


def dot_t(left, right):
    return lax.dot_general(left, right, (((1,), (1,)), ((), ())), preferred_element_type=F32)


def side_by_side(weights, windows):
    out = []
    for at in range(0, len(windows), 2):
        both = dot(weights, jnp.concatenate(windows[at : at + 2], 1))
        out += [both[:, 0:128], both[:, 128:256]]
    return out


def turned(block):
    return block.astype(F32).T.astype(BF16)


def swapped(block):
    return pltpu.roll(block.astype(F32), 64, 1).astype(BF16)


def sigmoid(values):
    return 1.0 / (1.0 + jnp.exp(-values))


def slope_of(values):
    sigma = sigmoid(values)
    return sigma * (1.0 + values * (1.0 - sigma))


def scenario_kernel(
    x_ref, w1_ref, w2_ref, w3_ref, w3b_ref, w2b_ref, regroup_ref, ftaps_ref, staps_ref, inter_ref,
    ow_ref, pc_ref,
    pred_ref, wire_ref,
    sums_ref, fx, stem_pre, mx, mid_pre, hx, hc_wide, hc_pad, mc_pair, mc_pad, sc_pad,
):
    lane = lax.broadcasted_iota(jnp.int32, (C2, 128), 1) % 64
    first, last = lane == 0, lane == 63

    def earlier(block):
        return jnp.where(first, 0.0, pltpu.roll(block, 1, 1))

    def later(block):
        return jnp.where(last, 0.0, pltpu.roll(block, 127, 1))

    lat = lax.broadcasted_iota(jnp.int32, (192, 128), 1)

    def load_slabs(at):
        places = [(s, half) for s in range(at, at + SLAB_BATCH) for half in (0, 1)]
        parts = [dot(regroup_ref[...], x_ref[s + 8 * half]).astype(BF16) for s, half in places]
        all_taps = dot(jnp.concatenate(parts, 0), ftaps_ref[...])
        for k, (s, half) in enumerate(places):
            taps = all_taps[192 * k : 192 * k + 192]
            even, odd = taps[:, 0:128], taps[:, 128:256]
            before = jnp.where(lat == 0, 0.0, pltpu.roll(odd, 1, 1))
            after = jnp.where(lat == 127, 0.0, pltpu.roll(even, 127, 1))
            wide = jnp.concatenate([t.reshape(SLAB_LON, CIN, 128) for t in (before, even, odd, after)], 1)
            rows = slice(1 + s * SLAB_LON, 1 + s * SLAB_LON + SLAB_LON)
            fx[rows, :, half * 128 : half * 128 + 128] = wide.astype(BF16)

    for at in range(0, 8, SLAB_BATCH):
        load_slabs(at)
    fx[0, :, 0:128] = fx[64, :, 128:256]
    fx[0, :, 128:256] = fx[64, :, 0:128]
    fx[65, :, 0:128] = fx[1, :, 128:256]
    fx[65, :, 128:256] = fx[1, :, 0:128]

    def stem(g):
        n = STEM_GROUP
        window = fx[pl.ds(2 * n * g, 2 * n + 2)].reshape((2 * n + 2) * 96, 256)
        pre = dot(w1_ref[...], window)
        stem_pre[n * g : n * g + n] = pre.reshape(n, C1, 256)
        return (pre * sigmoid(pre)).astype(BF16)

    def stem_taps(acts, at):
        n = STEM_GROUP * len(acts)
        taps = dot(jnp.concatenate(acts, 0), staps_ref[...])
        even, odd = taps[:, 0:128], taps[:, 128:256]
        lat = lax.broadcasted_iota(jnp.int32, odd.shape, 1) % 64
        before = jnp.where(lat == 0, 0.0, pltpu.roll(odd, 1, 1))
        wide = jnp.concatenate([t.reshape(n, C1, 128) for t in (before, even, odd)], 1)
        mx[1 + at : 1 + at + n] = wide.astype(BF16)

    for at in range(0, 32 // STEM_GROUP, STEM_BATCH):
        stem_taps([stem(at + k) for k in range(STEM_BATCH)], at * STEM_GROUP)
    mx[0] = swapped(mx[32])
    mx[33] = jnp.zeros((96, 128), BF16)

    def mid_window(g):
        n = MID_GROUP
        return mx[2 * n * g : 2 * n * g + 2 * n + 1].reshape((2 * n + 1) * 96, 128)

    def mid(g, pre):
        n = MID_GROUP
        mid_pre[n * g : n * g + n] = pre.reshape(n, C2, 128)
        act = pre * sigmoid(pre)
        for k in range(n):
            one = act[k * C2 : k * C2 + C2]
            hx[n * g + k + 1] = jnp.concatenate([earlier(one), one, later(one)], 0).astype(BF16)

    for step in range(0, 16 // MID_GROUP, 2):
        pres = side_by_side(w2_ref[...], [mid_window(step), mid_window(step + 1)])
        mid(step, pres[0])
        mid(step + 1, pres[1])
    hx[0] = swapped(hx[16])
    hx[17] = swapped(hx[1])

    for edge in (0, 1, 18, 19):
        hc_pad[edge] = jnp.zeros((C2, 128), BF16)
    out_w = jnp.broadcast_to(ow_ref[...], (C2, 128))

    def head_window(maps, g):
        n = HEAD_GROUP
        return maps[n * g : n * g + n + 2].reshape((n + 2) * 192, 128)

    def head(g, pre, out_sum):
        n = HEAD_GROUP
        sigma = sigmoid(pre)
        act = (pre * sigma).astype(BF16).astype(F32)
        bend = sigma * (1.0 + pre * (1.0 - sigma))
        for k in range(n):
            r = n * g + k
            here = slice(k * C2, k * C2 + C2)
            cot = jnp.broadcast_to(pc_ref[r : r + 1, :], (C2, 128))
            pred_ref[r : r + 1, :] = jnp.sum(out_w * act[here], 0, keepdims=True)
            out_sum = out_sum + cot * act[here]
            hc = (cot * out_w) * bend[here]
            hc_pad[r + 2] = hc.astype(BF16)
            hc_wide[r + 1] = jnp.concatenate([earlier(hc), hc, later(hc)], 0).astype(BF16)
        return out_sum

    out_sum = jnp.zeros((C2, 128), F32)
    for step in range(0, 16 // HEAD_GROUP, 2):
        pres = side_by_side(w3_ref[...], [head_window(hx, step), head_window(hx, step + 1)])
        out_sum = head(step, pres[0], out_sum)
        out_sum = head(step + 1, pres[1], out_sum)
    sums_ref[576:640, :] = out_sum
    hc_wide[0] = swapped(hc_wide[16])
    hc_wide[17] = swapped(hc_wide[1])

    for edge in (0, 17):
        mc_pad[edge] = jnp.zeros((C2, 128), BF16)

    def head_back(g, grad):
        n = HEAD_GROUP
        grad = grad.astype(BF16).astype(F32)
        mc = grad * slope_of(mid_pre[n * g : n * g + n].reshape(n * C2, 128))
        for k in range(n):
            one = mc[k * C2 : k * C2 + C2]
            mc_pad[n * g + k + 1] = one.astype(BF16)
            mc_pair[n * g + k] = jnp.concatenate([one, later(one)], 0).astype(BF16)

    for step in range(0, 16 // HEAD_GROUP, 2):
        grads = side_by_side(w3b_ref[...], [head_window(hc_wide, step), head_window(hc_wide, step + 1)])
        head_back(step, grads[0])
        head_back(step + 1, grads[1])
    mc_pair[16] = swapped(mc_pair[0])

    for edge in (0, 33):
        sc_pad[edge] = jnp.zeros((C1, 256), BF16)

    def mid_back(at):
        parts = []
        windows = [mc_pair[r : r + 2].reshape(256, 128) for r in range(at, at + BACK_BATCH)]
        for grad in side_by_side(w2b_ref[...], windows):
            grad = grad.astype(BF16)
            parts.append(jnp.concatenate([grad[0:64], grad[64:128]], 1))
        grads = dot(jnp.concatenate(parts, 0), inter_ref[...])
        for m in range(at // 2, (at + BACK_BATCH) // 2):
            grad = grads[128 * m - 64 * at : 128 * m - 64 * at + 128]
            cot = (grad * slope_of(stem_pre[4 * m : 4 * m + 4].reshape(128, 256))).astype(BF16)
            sc_pad[4 * m + 1 : 4 * m + 5] = cot.reshape(4, C1, 256)
            wire_ref[m, SHARE:WIRE_ROWS] = cot[:, 0:128]
            wire_ref[m + 8, SHARE:WIRE_ROWS] = cot[:, 128:256]

    for at in range(0, 16, BACK_BATCH):
        mid_back(at)

    total = None
    for k in range(0, 18, 2):
        left = jnp.concatenate([hc_pad[j : j + 3].reshape(192, 128) for j in (k, k + 1)], 1)
        right = jnp.concatenate([turned(hx[j]) for j in (k, k + 1)], 0)
        term = dot(left, right)
        total = term if total is None else total + term
    sums_ref[0:192, :] = total[:, 0:128]
    sums_ref[192:384, 0:64] = total[:, 128:192]
    total = None
    for k in range(17):
        term = dot_t(mx[2 * k : 2 * k + 2].reshape(192, 128), mc_pad[k : k + 2].reshape(128, 128))
        total = term if total is None else total + term
    sums_ref[384:576, :] = total
    total = None
    for k in range(33):
        term = dot(fx[2 * k : 2 * k + 2].reshape(192, 256), turned(sc_pad[k : k + 2].reshape(64, 256)))
        total = term if total is None else total + term
    sums_ref[192:384, 64:128] = total
    for s in range(SLABS):
        wire_ref[s, 0:SHARE] = sums_ref[s * SHARE : s * SHARE + SHARE, :].astype(BF16)


def scenario_pass(x, weights, out_weight, cotangent):
    out_shape = (
        jax.ShapeDtypeStruct((16, 128), F32),
        jax.ShapeDtypeStruct((SLABS, WIRE_ROWS, 128), BF16),
    )
    scratch = [
        pltpu.VMEM((SLABS * SHARE, 128), F32),
        pltpu.VMEM((66, 96, 256), BF16),
        pltpu.VMEM((32, C1, 256), F32),
        pltpu.VMEM((34, 96, 128), BF16),
        pltpu.VMEM((16, C2, 128), F32),
        pltpu.VMEM((18, 192, 128), BF16),
        pltpu.VMEM((18, 192, 128), BF16),
        pltpu.VMEM((20, C2, 128), BF16),
        pltpu.VMEM((17, 128, 128), BF16),
        pltpu.VMEM((18, C2, 128), BF16),
        pltpu.VMEM((34, C1, 256), BF16),
    ]
    whole = pl.BlockSpec(memory_space=pltpu.VMEM)
    return pl.pallas_call(
        scenario_kernel,
        out_shape=out_shape,
        in_specs=[whole] * 12,
        out_specs=(whole,) * 2,
        scratch_shapes=scratch,
        compiler_params=pltpu.CompilerParams(vmem_limit_bytes=32 << 20),
        cost_estimate=pl.CostEstimate(flops=4 * 10**9, bytes_accessed=4 << 20, transcendentals=10**6),
        name="scenario",
    )(x, *weights, *selections(), out_weight.reshape(C2, 1), cotangent)


def exchanged(value, axis, groups=None):
    return lax.all_to_all(
        value, axis, split_axis=0, concat_axis=0, tiled=True, axis_index_groups=groups
    )


def share_kernel(got_ref, out_ref):
    total = jnp.zeros((SHARE, 128), F32)
    for k in range(got_ref.shape[0]):
        total = total + got_ref[k, 0:SHARE].astype(F32)
    share = total.astype(BF16)
    for k in range(out_ref.shape[0]):
        out_ref[k] = share


def unpack_kernel(factor, sums_ref, stem_ref, mid_ref, head_ref, out_ref, wide):
    rows = SLABS * SHARE
    wide[...] = (sums_ref[0:rows].astype(F32) + sums_ref[rows : 2 * rows].astype(F32)) * factor
    for a in range(3):
        at = (2 - a) * C2
        head_ref[a, 0] = wide[at : at + C2, 0:64]
        head_ref[a, 1] = wide[at : at + C2, 64:128]
        head_ref[a, 2] = wide[192 + at : 192 + at + C2, 0:64]
        lanes = slice(0, 64) if a == 2 else slice(64, 128)
        for b in range(3):
            at = 384 + a % 2 * 96 + b * C1
            mid_ref[a, b] = wide[at : at + C1, lanes]
    for a in range(4):
        lanes = slice(64, 96) if a >= 2 else slice(96, 128)
        for c in range(CIN):
            taps = wide[pl.ds(192 + a % 2 * 96 + c, 4, stride=CIN), :]
            stem_ref[c, a] = taps[:, lanes]
    ones = jnp.full((8, 128), 1.0, BF16)
    out_sums = [dot_t(ones, sums_ref[at + 576 : at + 640])[0:1] for at in (0, rows)]
    out_ref[...] = (out_sums[0] + out_sums[1]) * factor


def on_chip(kernel, outs, scratch=(), name=None):
    whole = pl.BlockSpec(memory_space=pltpu.VMEM)
    single = not isinstance(outs, tuple)
    return lambda *args: pl.pallas_call(
        kernel,
        out_shape=outs,
        in_specs=[whole] * len(args),
        out_specs=whole if single else (whole,) * len(outs),
        scratch_shapes=scratch,
        compiler_params=pltpu.CompilerParams(vmem_limit_bytes=8 << 20),
        name=name,
    )(*args)


def summed_everywhere(got, factor):
    lon, rep = lax.axis_size("lon"), lax.axis_size("rep")
    lines = [list(range(parity, rep, 2)) for parity in (0, 1)]
    planes = [
        [(2 * z + parity) * lon + k for parity in (0, 1) for k in range(lon)] for z in range(rep // 2)
    ]
    one_line = jax.ShapeDtypeStruct((rep // 2, SHARE, 128), BF16)
    one_plane = jax.ShapeDtypeStruct((2 * lon, SHARE, 128), BF16)
    share = on_chip(share_kernel, one_line, name="lon_share")(got)
    share = on_chip(share_kernel, one_plane, name="line_share")(exchanged(share, "rep", lines))
    sums = exchanged(share, ("rep", "lon"), planes).reshape(2 * SLABS * SHARE, 128)
    outs = (
        jax.ShapeDtypeStruct((CIN, 4, 4, C1), F32),
        jax.ShapeDtypeStruct((3, 3, C1, C2), F32),
        jax.ShapeDtypeStruct((3, 3, C2, C2), F32),
        jax.ShapeDtypeStruct((1, C2), F32),
    )
    scratch = [pltpu.VMEM((SLABS * SHARE, 128), F32)]
    stem, mid, head, out = on_chip(functools.partial(unpack_kernel, factor), outs, scratch, "unpack")(sums)
    return stem.transpose(3, 0, 1, 2), mid.transpose(3, 2, 0, 1), head.transpose(2, 3, 0, 1), out.reshape(C2)


def local(fields, stem_weight, mid_weight, head_weight, out_weight, pred_cotangent):
    x = exchanged(fields.reshape(SLABS, CIN * SLAB_LON, LAT), "lon")
    weights = kernel_weights(stem_weight, mid_weight, head_weight)
    cotangent = pred_cotangent.reshape(2, 16, 64).transpose(1, 0, 2).reshape(16, 128)
    prediction, wire = scenario_pass(x, weights, out_weight, cotangent)
    prediction = prediction.reshape(16, 2, 64).transpose(1, 0, 2).reshape(1, 32, 64)
    got = exchanged(wire, "lon")
    stem_cotangent = got[:, SHARE:].reshape(SLABS, 4, C1, 128).transpose(0, 2, 1, 3)
    factor = 1.0 / (fields.shape[0] * lax.axis_size("rep"))
    return (prediction, stem_cotangent, *summed_everywhere(got, factor))


def solution(mesh):
    placed = (P("rep", None, "lon", None), P(), P(), P(), P(), P(("rep", "lon"), None, None))
    return jax.shard_map(
        local,
        mesh=mesh,
        in_specs=placed,
        out_specs=(P(("rep", "lon"), None, None), P("rep", None, "lon", None), P(), P(), P(), P()),
        check_vma=False,
    )
```
